32 devices in a mesh: grp: 2 (over x), dev: 16 (over z, y, core).
Axes of the slice: x: 2, y: 2, z: 4, core: 2. Of those that a mesh axis runs over, the one named last changes fastest.
Arguments:
- coords: float32 [16384, 64], P(('grp', 'dev')), may hold values from -6 to 6
- right_side: float32 [16384, 256], P(('grp', 'dev')), may hold values from -6 to 6
- leaf_perm: int32 [32, 512], P(('grp', 'dev')), may hold values from 0 to 511, each once within a row
- near_list: int32 [32, 4], P(('grp', 'dev')), may hold values from -1 to 31, as said below
- far_leaves: int32 [32, 4], P(('grp', 'dev')), may hold values from 0 to 31, as said below
- couplings: bfloat16 [32, 4, 128, 128], P(('grp', 'dev')), may hold values from -0.5 to 0.5
- transfer: bfloat16 [32, 128, 128], P(('grp', 'dev')), may hold values from -0.5 to 0.5
- leaf_basis: bfloat16 [16384, 128], P(('grp', 'dev')), may hold values from -0.25 to 0.25
- cluster_of: int32 [32], P(('grp', 'dev')), may hold values from 0 to 7, as said below
- far_clusters: int32 [8, 4], P('grp'), may hold values from 0 to 7, as said below
- cluster_couplings: bfloat16 [8, 4, 128, 128], P('grp'), may hold values from -0.25 to 0.25
- ridge_weight: float32 [], replicated, may hold values from 0.5 to 2
Outputs:
- solution: float32 [16384, 256], P(('grp', 'dev'))
- residual: float32 [16384, 256], P(('grp', 'dev'))
The draws below stay inside these ranges and needn't reach their ends.
Inputs may be any that keep to these rules, and one draw needn't show every extreme that they name: `near_list`: each row lists leaves of the row's group whose position within the group differs from the row's leaf by 1 to 2, each at most once, in any slot order; -1 marks an empty slot. The number of listed leaves varies from leaf to leaf. `far_leaves`: each row names 4 different leaves of the row's group whose position within the group differs from the row's leaf by more than 2 and at most 8. `cluster_of`: leaves of group g belong to clusters g * 4 to g * 4 + 3, and every cluster holds exactly 4 leaves. `far_clusters`: each row names 4 different clusters, none of them in the row's own group.
All inputs are finite; a program needn't handle non-finite values.
Results may differ from the reference program's by a relative error of at most 0.0033.
Values may be sent and summed in bfloat16 or wider, within the bound.
A program may use at most 64 MiB of HBM per device.

```python
import jax
import jax.numpy as jnp
from jax import lax

LEAF = 512
DIM = 64
OUT = 256
RANK = 128
REACH = 2
FARREACH = 8
FAR1 = 4
FAR2 = 4
CPG = 4
ITERS = 2
LEAVES = 32
POINTS = 16384
CLUS = 8
LPC = 4
N_GRP = 2
N_DEV = 16


def draw_near_list(key, part):
    count_all = N_GRP * N_DEV
    offset_table = jnp.concatenate([jnp.arange(-REACH, 0), jnp.arange(1, REACH + 1)]).astype(jnp.int32)
    subkeys = jax.random.split(key, 3)
    orders = jax.vmap(lambda single: jax.random.permutation(single, 2 * REACH))(jax.random.split(subkeys[0], count_all))
    offsets = offset_table[orders]
    keep_level = jax.random.randint(subkeys[1], (count_all, 1), 1, 5)
    coin_draws = jax.random.randint(subkeys[2], (count_all, 2 * REACH), 0, 4)
    leaf_index = jnp.arange(count_all, dtype=jnp.int32)[:, None]
    position = leaf_index % N_DEV + offsets
    retained = (coin_draws < keep_level) & (position >= 0) & (position < N_DEV)
    return jnp.where(retained, leaf_index + offsets, -1).astype(jnp.int32)


def draw_far_leaves(key, part):
    count_all = N_GRP * N_DEV
    orders = jax.vmap(lambda single: jax.random.permutation(single, N_DEV))(jax.random.split(jax.random.fold_in(key, 11), count_all))
    leaf_index = jnp.arange(count_all, dtype=jnp.int32)[:, None]
    offset = orders - leaf_index % N_DEV
    allowed = (jnp.abs(offset) > REACH) & (jnp.abs(offset) <= FARREACH)
    ranking = jnp.where(allowed, 0, N_DEV) + jnp.arange(N_DEV, dtype=jnp.int32)[None, :]
    chosen = jnp.argsort(ranking, axis=1)[:, :FAR1]
    picked = jnp.take_along_axis(orders, chosen, axis=1)
    return (leaf_index // N_DEV * N_DEV + picked).astype(jnp.int32)


def draw_cluster_of(key, part):
    per_cluster = N_DEV // CPG
    orders = jax.vmap(lambda single: jax.random.permutation(single, N_DEV))(jax.random.split(jax.random.fold_in(key, 23), N_GRP))
    group_index = jnp.arange(N_GRP, dtype=jnp.int32)[:, None]
    return (group_index * CPG + orders // per_cluster).reshape(N_GRP * N_DEV).astype(jnp.int32)


def draw_far_clusters(key, part):
    count_all = N_GRP * CPG
    orders = jax.vmap(lambda single: jax.random.permutation(single, count_all))(jax.random.split(jax.random.fold_in(key, 37), count_all))
    cluster_index = jnp.arange(count_all, dtype=jnp.int32)[:, None]
    allowed = orders // CPG != cluster_index // CPG
    ranking = jnp.where(allowed, 0, count_all) + jnp.arange(count_all, dtype=jnp.int32)[None, :]
    chosen = jnp.argsort(ranking, axis=1)[:, :FAR2]
    return jnp.take_along_axis(orders, chosen, axis=1).astype(jnp.int32)


def shard_levels(stream_key, extent, cuts, low, largest):
    def one(axis_at, blocks):
        draws = jax.random.uniform(jax.random.fold_in(jax.random.fold_in(stream_key, 6), axis_at), (blocks,), jnp.float32, low / len(cuts), largest / len(cuts))
        return jnp.repeat(jnp.exp(draws), extent[axis_at] // blocks).reshape((-1,) + (1,) * (len(extent) - axis_at - 1))

    level = one(*cuts[0])
    for cut in cuts[1:]:
        level = level * one(*cut)
    return level


def gaussian(key, shape, width, limit, shards=(), held_as=jnp.bfloat16):
    drawn = jax.random.normal(key, shape, jnp.float32) * width
    if len(shards) > 0:
        drawn = shard_levels(key, shape, shards, -0.22, 0.18) * drawn
    return jnp.clip(drawn, min=-limit, max=limit).astype(held_as)


def setup_inputs(seed: int = 0) -> dict:
    streams_of = jax.random.split(jax.random.key(seed), 13)
    return {
        "coords": gaussian(streams_of[0], (POINTS, DIM), 1.0, 6.0, ((0, 32),), jnp.float32),
        "right_side": gaussian(streams_of[1], (POINTS, OUT), 1.0, 6.0, ((0, 32),), jnp.float32),
        "leaf_perm": jax.vmap(lambda own: jax.random.permutation(own, LEAF))(jax.random.split(streams_of[2], LEAVES)).reshape((LEAVES, LEAF)).astype(jnp.int32),
        "near_list": draw_near_list(jax.random.fold_in(streams_of[12], 71), 0),
        "far_leaves": draw_far_leaves(jax.random.fold_in(streams_of[12], 71), 0),
        "couplings": gaussian(streams_of[5], (LEAVES, FAR1, RANK, RANK), RANK ** -0.5, 0.5, ((0, 32),)),
        "transfer": gaussian(streams_of[6], (LEAVES, RANK, RANK), RANK ** -0.5, 0.5, ((0, 32),)),
        "leaf_basis": gaussian(streams_of[7], (POINTS, RANK), LEAF ** -0.5, 0.25, ((0, 32),)),
        "cluster_of": draw_cluster_of(jax.random.fold_in(streams_of[12], 71), 0),
        "far_clusters": draw_far_clusters(jax.random.fold_in(streams_of[12], 71), 0),
        "cluster_couplings": gaussian(streams_of[10], (CLUS, FAR2, RANK, RANK), (RANK * LPC) ** -0.5, 0.25, ((0, 2),)),
        "ridge_weight": jnp.clip(jax.random.uniform(streams_of[11], (), jnp.float32, 0.5, 2.0), 0.5, 2.0),
    }


kernel_scale = 1.0 / 32.0
spectrum_gap = 0.5
spectrum_top = 8.0


def kernel_block(left_points, right_points):
    inner_products = jnp.dot(left_points, right_points.T, precision=lax.Precision.HIGHEST, preferred_element_type=jnp.float32)
    distance = jnp.sum(left_points * left_points, axis=1)[:, None] + jnp.sum(right_points * right_points, axis=1)[None, :] - 2.0 * inner_products
    return jnp.exp(-kernel_scale * distance).astype(jnp.bfloat16)


def place_back(tree_rows, ordering):
    return jnp.zeros_like(tree_rows).at[ordering].set(tree_rows)


def apply_operator(direction, coords, leaf_perm, near_list, far_leaves, couplings, transfer, leaf_basis, cluster_of, far_clusters, cluster_couplings, ridge_weight):
    values = direction.astype(jnp.bfloat16).reshape(LEAVES, LEAF, OUT)
    points = coords.reshape(LEAVES, LEAF, DIM)

    def near_leaf(leaf_id):
        own_points = points[leaf_id]
        accumulated = jnp.dot(kernel_block(own_points, own_points), values[leaf_id], preferred_element_type=jnp.float32)
        for offset in list(range(-REACH, 0)) + list(range(1, REACH + 1)):
            neighbour = jnp.clip(leaf_id + offset, 0, LEAVES - 1)
            listed = jnp.any((near_list[leaf_id] == leaf_id + offset) & (near_list[leaf_id] >= 0)).astype(jnp.float32)
            accumulated = accumulated + listed * jnp.dot(kernel_block(own_points, points[neighbour]), values[neighbour], preferred_element_type=jnp.float32)
        return accumulated

    near_field = lax.map(near_leaf, jnp.arange(LEAVES, dtype=jnp.int32))
    ordered = jnp.take_along_axis(values, leaf_perm[:, :, None], axis=1)
    leaf_bases = leaf_basis.reshape(LEAVES, LEAF, RANK).astype(jnp.float32)
    skeleton = jnp.einsum('lpa,lpo->lao', leaf_bases, ordered.astype(jnp.float32)).astype(jnp.bfloat16)
    transfer_wide = transfer.astype(jnp.float32)
    uplift = jnp.einsum('lba,lbo->lao', transfer_wide, skeleton.astype(jnp.float32))
    cluster_sums = jnp.zeros((CLUS, RANK, OUT), jnp.float32).at[cluster_of].add(uplift).astype(jnp.bfloat16)
    picked = cluster_sums[far_clusters]
    coupled = jnp.einsum('ckab,ckbo->cao', cluster_couplings.astype(jnp.float32), picked.astype(jnp.float32)).astype(jnp.bfloat16)
    partners = skeleton[far_leaves]
    level_one = jnp.einsum('lkab,lkbo->lao', couplings.astype(jnp.float32), partners.astype(jnp.float32))
    local_sum = level_one + jnp.einsum('lab,lbo->lao', transfer_wide, coupled[cluster_of].astype(jnp.float32))
    tree_rows = jnp.einsum('lpa,lao->lpo', leaf_bases, local_sum.astype(jnp.bfloat16).astype(jnp.float32))
    far_field = jax.vmap(place_back)(tree_rows, leaf_perm)
    return ridge_weight * direction + (near_field + far_field).reshape(LEAVES * LEAF, OUT)


def reference(coords, right_side, leaf_perm, near_list, far_leaves, couplings, transfer, leaf_basis, cluster_of, far_clusters, cluster_couplings, ridge_weight):
    bottom_edge = ridge_weight + spectrum_gap
    top_edge = ridge_weight + spectrum_top
    centre = (top_edge + bottom_edge) / 2.0
    spread = (top_edge - bottom_edge) / 2.0
    sigma_ratio = centre / spread
    contraction = 1.0 / sigma_ratio
    direction = right_side / centre
    solution = direction
    residual = right_side
    for rounds in range(ITERS):
        residual = residual - apply_operator(direction, coords, leaf_perm, near_list, far_leaves, couplings, transfer, leaf_basis, cluster_of, far_clusters, cluster_couplings, ridge_weight)
        rho_next = 1.0 / (2.0 * sigma_ratio - contraction)
        direction = rho_next * contraction * direction + (2.0 * rho_next / spread) * residual
        solution = solution + direction
        contraction = rho_next
    return solution, residual
```

```python
import functools

import jax
import jax.numpy as jnp
from jax import lax
from jax.experimental import pallas as pl
from jax.experimental.pallas import tpu as pltpu
from jax.sharding import PartitionSpec as P

MESH = pl.DeviceIdType.MESH
PARTS = 2
EARLY = 1

REACH = 2
FARREACH = 8
ITERS = 2


kernel_scale = 1.0 / 32.0
spectrum_gap = 0.5
spectrum_top = 8.0


def from_behind(shard, axis, by):
    devices = lax.axis_size(axis)
    pairs = [(i, i + by) for i in range(devices) if 0 <= i + by < devices]
    return lax.ppermute(shard, axis, pairs)


def kernel_block(left_points, right_points):
    inner_products = jnp.dot(
        left_points,
        right_points.T,
        precision=lax.Precision.HIGHEST,
        preferred_element_type=jnp.float32,
    )
    distance = (
        jnp.sum(left_points * left_points, axis=1)[:, None]
        + jnp.sum(right_points * right_points, axis=1)[None, :]
        - 2.0 * inner_products
    )
    return jnp.exp(-kernel_scale * distance).astype(jnp.bfloat16)


def body(
    coords,
    right_side,
    leaf_perm,
    near_list,
    far_leaves,
    couplings,
    transfer,
    leaf_basis,
    cluster_of,
    far_clusters,
    cluster_couplings,
    ridge_weight,
):
    dev_count = lax.axis_size("dev")
    group_index = lax.axis_index("grp")
    leaf_id = group_index * dev_count + lax.axis_index("dev")
    clusters_here = far_clusters.shape[0]
    local_cluster = cluster_of[0] - group_index * clusters_here
    ordering = leaf_perm[0]
    near_offsets = [offset for offset in range(-REACH, REACH + 1) if offset != 0]
    far_offsets = [offset for offset in range(-FARREACH, FARREACH + 1) if abs(offset) > REACH]
    neighbours = [from_behind(coords, "dev", -offset) for offset in near_offsets]
    near_flags = [
        jnp.any((near_list[0] == leaf_id + offset) & (near_list[0] >= 0)).astype(jnp.float32)
        for offset in near_offsets
    ]
    far_hits = jnp.stack(
        [far_leaves[0] == leaf_id + offset for offset in far_offsets], axis=1
    ).astype(jnp.bfloat16)
    own_block = kernel_block(coords, coords)
    near_blocks = [kernel_block(coords, neighbour_points) for neighbour_points in neighbours]
    cluster_slots = (jnp.arange(clusters_here) == local_cluster).astype(jnp.float32)

    def operate(direction):
        values = direction.astype(jnp.bfloat16)
        near_sum = jnp.dot(own_block, values, preferred_element_type=jnp.float32)
        for position in range(len(near_offsets)):
            remote = from_behind(values, "dev", -near_offsets[position])
            block_here = near_blocks[position]
            near_term = near_flags[position] * jnp.dot(
                block_here, remote, preferred_element_type=jnp.float32
            )
            near_sum = near_sum + near_term
        skeleton = lax.dot_general(
            leaf_basis,
            values[ordering],
            (((0,), (0,)), ((), ())),
            preferred_element_type=jnp.float32,
        ).astype(jnp.bfloat16)
        remote_skeletons = jnp.stack(
            [from_behind(skeleton, "dev", -offset) for offset in far_offsets]
        )
        chosen = jnp.einsum(
            "kj,jbo->kbo", far_hits, remote_skeletons, preferred_element_type=jnp.float32
        ).astype(jnp.bfloat16)
        level_one = jnp.einsum(
            "kab,kbo->ao", couplings[0], chosen, preferred_element_type=jnp.float32
        )
        uplift = lax.dot_general(
            transfer[0], skeleton, (((0,), (0,)), ((), ())), preferred_element_type=jnp.float32
        )
        contrib = cluster_slots[:, None, None] * uplift[None]
        column_sums = lax.psum_scatter(contrib, "dev", scatter_dimension=2, tiled=True).astype(
            jnp.bfloat16
        )
        every_column = lax.all_gather(column_sums, "grp", axis=0, tiled=True)
        picked = every_column[far_clusters]
        partial_coupled = jnp.einsum(
            "ckab,ckbo->cao", cluster_couplings, picked, preferred_element_type=jnp.float32
        ).astype(jnp.bfloat16)
        whole_columns = lax.all_gather(partial_coupled, "dev", axis=2, tiled=True)
        coupled = whole_columns[local_cluster]
        downward = jnp.dot(transfer[0], coupled, preferred_element_type=jnp.float32)
        tree_rows = jnp.dot(
            leaf_basis,
            (level_one + downward).astype(jnp.bfloat16),
            preferred_element_type=jnp.float32,
        )
        far_part = jnp.zeros_like(tree_rows).at[ordering].set(tree_rows)
        return ridge_weight * direction + (near_sum + far_part)

    bottom_edge = ridge_weight + spectrum_gap
    top_edge = ridge_weight + spectrum_top
    centre = (top_edge + bottom_edge) / 2.0
    spread = (top_edge - bottom_edge) / 2.0
    sigma_ratio = centre / spread
    contraction = 1.0 / sigma_ratio
    direction = right_side / centre
    solution = direction
    residual = right_side
    for rounds in range(ITERS):
        residual = residual - operate(direction)
        rho_next = 1.0 / (2.0 * sigma_ratio - contraction)
        direction = rho_next * contraction * direction + 2.0 * rho_next / spread * residual
        solution = solution + direction
        contraction = rho_next
    return (solution, residual)


def fused_kernel(
    n,
    coords_hbm,
    right_hbm,
    perm_hbm,
    near_hbm,
    far_hbm,
    coup_hbm,
    transfer_hbm,
    basis_hbm,
    cluster_ref,
    farclus_hbm,
    cluscoup_hbm,
    ridge_hbm,
    sol_ref,
    res_ref,
    points,
    wide,
    blocks,
    skel,
    up_out,
    up_in,
    tag_in,
    sums_t,
    pair_map,
    partners,
    c_out,
    c_in,
    basis_p,
    basis_t,
    acc,
    direction,
    perm_ref,
    basis_ref,
    transfer_ref,
    coup_ref,
    cluscoup_ref,
    ridge_ref,
    near_ref,
    far_ref,
    farclus_ref,
    load_sem,
    near_send,
    near_recv,
    tree_send,
    tree_recv,
    wide_send,
    wide_recv,
):
    f32, bf16 = jnp.float32, jnp.bfloat16
    group = lax.axis_index("grp")
    me = lax.axis_index("dev")
    other = 1 - group
    chip = lax.div(me, 2)
    core = lax.rem(me, 2)
    row = lax.rem(chip, 2)
    mate = chip * 2 + (1 - core)
    across = me + 2 - 4 * row
    across_mate = mate + 2 - 4 * row
    leaf, outs = right_hbm.shape
    dim = coords_hbm.shape[0]
    rank = transfer_hbm.shape[1]
    clusters = cluscoup_hbm.shape[0]
    width = outs // n
    tag_rows = 16
    has_z = ((row == 0) & (me >= 4)) | ((row == 1) & (me + 4 < n))
    sends_z = ((row == 0) & (me + 4 < n)) | ((row == 1) & (me >= 4))
    z_target = jnp.where(sends_z, me + 4 - 8 * row, me)

    barrier = pltpu.get_barrier_semaphore()
    for step in range(n):
        place = lax.rem(me + step, n)
        pl.semaphore_signal(
            barrier, inc=1, device_id={"grp": other, "dev": place}, device_id_type=MESH
        )
        if step > 0:
            pl.semaphore_signal(barrier, inc=1, device_id={"dev": place}, device_id_type=MESH)

    loads = {}
    for name, source, target in (
        ("perm", perm_hbm, perm_ref),
        ("basis", basis_hbm, basis_ref),
        ("ridge", ridge_hbm, ridge_ref),
        ("right", right_hbm, res_ref),
        ("transfer", transfer_hbm, transfer_ref),
        ("coords", coords_hbm, points.at[pl.ds(0, dim)]),
        ("near", near_hbm, near_ref),
        ("far", far_hbm, far_ref),
        ("farclus", farclus_hbm, farclus_ref),
        ("cluscoup", cluscoup_hbm, cluscoup_ref),
        ("coup", coup_hbm, coup_ref),
    ):
        loads[name] = pltpu.make_async_copy(source, target, load_sem.at[len(loads)])
        loads[name].start()

    def near_copy(buf, stage, source, slot, target, size, part):
        piece = size // PARTS
        return pltpu.make_async_remote_copy(
            src_ref=buf.at[pl.ds(source * size + part * piece, piece)],
            dst_ref=buf.at[pl.ds(slot * size + part * piece, piece)],
            send_sem=near_send.at[stage, slot, part],
            recv_sem=near_recv.at[stage, slot, part],
            device_id={"dev": target},
            device_id_type=MESH,
        )

    def near_start(buf, stage, size):
        for part in range(PARTS):
            near_copy(buf, stage, 0, 2, across, size, part).start()
        for part in range(PARTS):
            near_copy(buf, stage, 0, 1, mate, size, part).start()

        @pl.when(jnp.logical_not(has_z))
        def _():
            buf[pl.ds(3 * size, size), :] = jnp.zeros((size, buf.shape[1]), buf.dtype)

        @pl.when(jnp.logical_not(has_z) & (core == row))
        def _():
            buf[pl.ds(4 * size, size), :] = jnp.zeros((size, buf.shape[1]), buf.dtype)

    def near_relay(buf, stage, size, parts):
        for part in parts:
            near_copy(buf, stage, 0, 2, across, size, part).wait_recv()

            @pl.when(sends_z)
            def _():
                near_copy(buf, stage, 2, 3, z_target, size, part).start()

            @pl.when(core == row)
            def _():
                near_copy(buf, stage, 2, 4, mate, size, part).start()

    def near_second(buf, stage, size):
        for part in range(PARTS):

            @pl.when(has_z)
            def _():
                near_copy(buf, stage, 2, 3, mate, size, part).wait_recv()

            @pl.when(has_z & (core != row))
            def _():
                near_copy(buf, stage, 3, 4, mate, size, part).start()

    def near_first(buf, stage, size):
        for part in range(PARTS):
            near_copy(buf, stage, 0, 1, mate, size, part).wait_recv()

    def near_finish(buf, stage, size):
        for part in range(PARTS):

            @pl.when(has_z | (core != row))
            def _():
                near_copy(buf, stage, 0, 4, mate, size, part).wait_recv()

    def near_drain(buf, stage, size):
        for part in range(PARTS):
            near_copy(buf, stage, 0, 1, mate, size, part).wait_send()
            near_copy(buf, stage, 0, 2, across, size, part).wait_send()

            @pl.when(sends_z)
            def _():
                near_copy(buf, stage, 2, 3, z_target, size, part).wait_send()

            @pl.when(has_z | (core == row))
            def _():
                near_copy(buf, stage, 0, 4, mate, size, part).wait_send()

    heading = 1 - 2 * row

    def inside(owner):
        return (owner >= 0) & (owner < n)

    def tree_copy(rounds, step, owner, target):
        owner = jnp.clip(owner, 0, n - 1)
        place = pl.ds(pl.multiple_of(owner * rank, 16), rank)
        return pltpu.make_async_remote_copy(
            src_ref=skel.at[rounds, place],
            dst_ref=skel.at[rounds, place],
            send_sem=tree_send.at[rounds, step],
            recv_sem=tree_recv.at[rounds, owner],
            device_id={"dev": jnp.clip(target, 0, n - 1)},
            device_id_type=MESH,
        )

    along = (1, -1, 2, -2)
    own_sends = [(inside(me + 4 * dz), me, me + 4 * dz) for dz in along]
    own_sends.append((core == row, me, across_mate))
    lane_waits, lane_sends = [], []
    for dz in along:
        owner = me - 4 * dz
        here = inside(owner)
        lane_waits.append((here, owner))
        passes = here
        if dz == 2:
            passes = here & (core == 1)
        if dz == -2:
            passes = here & (core == 0)
        full = (heading == dz) | (heading * -2 == dz)
        part = (heading == -dz) & (core == 1 - row)
        lane_sends.append(
            [(passes, owner, mate), (here & (full | part), owner, jnp.where(part, across_mate, across))]
        )
    side_waits = [
        (inside(across + 4 * heading), across + 4 * heading),
        (inside(across - 8 * heading), across - 8 * heading),
    ]
    side_sends = [(here, owner, mate) for here, owner in side_waits]
    last_waits = [
        (core == row, across_mate),
        ((core == 1 - row) & inside(across_mate - 4 * heading), across_mate - 4 * heading),
        (inside(mate - 4), mate - 4),
        (inside(mate + 4), mate + 4),
        ((core == 0) & inside(mate - 8), mate - 8),
        ((core == 1) & inside(mate + 8), mate + 8),
        (inside(across_mate + 4 * heading), across_mate + 4 * heading),
        (inside(across_mate - 8 * heading), across_mate - 8 * heading),
    ]
    every_send = own_sends + [pair for pairs in lane_sends for pair in pairs] + side_sends

    def tree_go(rounds, first, sends):
        for step, (when, owner, target) in enumerate(sends):

            @pl.when(when)
            def _():
                tree_copy(rounds, first + step, owner, target).start()

    def tree_wait(rounds, waits):
        for when, owner in waits:

            @pl.when(when)
            def _():
                tree_copy(rounds, 0, owner, mate).wait_recv()

    def tree_lanes(rounds, chosen):
        for lane in chosen:
            tree_wait(rounds, lane_waits[lane : lane + 1])
            tree_go(rounds, len(own_sends) + 2 * lane, lane_sends[lane])

    def tree_sides(rounds):
        for side in range(2):
            tree_wait(rounds, side_waits[side : side + 1])
            tree_go(rounds, len(every_send) - 2 + side, side_sends[side : side + 1])

    def tree_drain(rounds):
        for step, (when, owner, target) in enumerate(every_send):

            @pl.when(when)
            def _():
                tree_copy(rounds, step, owner, target).wait_send()

    def wide_copy(source, target, sem, device):
        return pltpu.make_async_remote_copy(
            src_ref=source,
            dst_ref=target,
            send_sem=wide_send.at[sem],
            recv_sem=wide_recv.at[sem],
            device_id=device,
            device_id_type=MESH,
        )

    def up_rows(rounds):
        return width + tag_rows if rounds == 0 else width

    def up_start(rounds):
        for step in range(n):
            place = lax.rem(me + n // 2 + step, n)
            rows = pl.ds(0, up_rows(rounds))
            wide_copy(
                up_out.at[rounds, place, rows],
                up_in.at[rounds, me, rows],
                rounds,
                {"grp": other, "dev": place},
            ).start()

    def up_all(rounds):
        whole = up_in.at[rounds, pl.ds(0, n), pl.ds(0, up_rows(rounds))]
        return wide_copy(whole, whole, rounds, {"grp": other})

    def tag_start():
        for step in range(1, n):
            place = lax.rem(me + step, n)
            wide_copy(tag_in.at[me], tag_in.at[me], ITERS, {"dev": place}).start()

    def tag_all():
        whole = tag_in.at[pl.ds(0, n - 1)]
        return wide_copy(whole, whole, ITERS, {"dev": mate})

    def down_start(rounds):
        for step in range(1, n):
            place = lax.rem(me + step, n)
            wide_copy(
                c_out.at[rounds, place],
                c_in.at[rounds, me],
                ITERS + 1 + rounds,
                {"dev": place},
            ).start()

    def down_all(rounds):
        whole = c_in.at[rounds, pl.ds(0, n - 1)]
        return wide_copy(whole, whole, ITERS + 1 + rounds, {"dev": mate})

    local_cluster = cluster_ref[0] - group * clusters
    lane_rows = lax.broadcasted_iota(jnp.int32, (tag_rows, rank), 0)
    tags = jnp.where(lane_rows == local_cluster, 1.0, 0.0).astype(bf16)
    tag_in[me] = tags
    for place in range(n):
        up_out[0, place, width:, :] = tags

    loads["perm"].wait()
    targets = lax.broadcasted_iota(jnp.int32, (leaf, leaf), 0)
    one_hot = jnp.where(targets == perm_ref[...], 1.0, 0.0).astype(bf16)
    loads["basis"].wait()
    placed = jnp.dot(one_hot, basis_ref[...], preferred_element_type=f32)
    basis_p[...] = placed.astype(bf16)
    basis_t[...] = placed.T.astype(bf16)
    loads["ridge"].wait()
    ridge = ridge_ref[...]
    bottom_edge = ridge + spectrum_gap
    top_edge = ridge + spectrum_top
    centre = (top_edge + bottom_edge) / 2.0
    spread = (top_edge - bottom_edge) / 2.0
    sigma_ratio = centre / spread
    contraction = 1.0 / sigma_ratio
    loads["right"].wait()
    start = res_ref[...] / centre
    direction[...] = start
    sol_ref[...] = start
    loads["transfer"].wait()
    transfer_rows = transfer_ref[0]

    def prepare(rounds):
        values = direction[...].astype(bf16)
        wide[rounds, pl.ds(0, leaf), :] = values
        skeleton = jnp.dot(basis_t[...], values, preferred_element_type=f32)
        skel[rounds, pl.ds(pl.multiple_of(me * rank, 16), rank), :] = skeleton.astype(bf16)
        uplift = jnp.dot(
            skeleton.T.astype(bf16), transfer_rows, preferred_element_type=f32
        ).astype(bf16)
        for place in range(n):
            up_out[rounds, place, 0:width, :] = uplift[place * width : (place + 1) * width, :]

    def send(rounds):
        up_start(rounds)
        near_start(wide.at[rounds], rounds + 1, leaf)
        tree_go(rounds, 0, own_sends)

    def map_clusters():
        for c in range(clusters):
            for place in range(clusters):
                total = jnp.zeros((rank, rank), f32)
                for k in range(farclus_ref.shape[1]):
                    hit = (farclus_ref[c, k] == other * clusters + place).astype(f32)
                    total = total + hit * cluscoup_ref[c, k].astype(f32)
                pair_map[place * rank : (place + 1) * rank, c * rank : (c + 1) * rank] = (
                    total.T.astype(bf16)
                )

    def map_partners():
        for place in range(n):
            total = jnp.zeros((rank, rank), f32)
            for k in range(far_ref.shape[1]):
                hit = (far_ref[0, k] == group * n + place).astype(f32)
                total = total + hit * coup_ref[0, k].astype(f32)
            partners[:, place * rank : (place + 1) * rank] = total.astype(bf16)

            @pl.when((jnp.abs(me - place) <= REACH) | (jnp.abs(me - place) > FARREACH))
            def _():
                for rounds in range(ITERS):
                    if rounds > 0 :
                        skel[rounds, place * rank : (place + 1) * rank, :] = jnp.zeros(
                            (rank, outs), bf16
                        )

                @pl.when(me != place)
                def _():
                    skel[0, place * rank : (place + 1) * rank, :] = jnp.zeros((rank, outs), bf16)

    def couple(rounds):
        up_all(rounds).wait_recv()
        totals = [jnp.zeros((width, rank), f32) for _ in range(clusters)]
        for place in range(n):
            part = up_in[rounds, place, 0:width, :].astype(f32)
            tag = up_in[0, place, width:, :].astype(f32)
            totals = [totals[c] + tag[c : c + 1, :] * part for c in range(clusters)]
        for c in range(clusters):
            sums_t[:, c * rank : (c + 1) * rank] = totals[c].astype(bf16)
        coupled = jnp.dot(sums_t[...], pair_map[...], preferred_element_type=f32)
        coupled = coupled.astype(bf16).astype(f32)
        if rounds == 0:
            tag_all().wait_recv()
        for place in range(n):
            tag = tag_in[place].astype(f32)
            pick = jnp.zeros((width, rank), f32)
            for c in range(clusters):
                pick = pick + tag[c : c + 1, :] * coupled[:, c * rank : (c + 1) * rank]
            c_out[rounds, place] = pick.astype(bf16)
        c_in[rounds, me] = c_out[rounds, me]
        down_start(rounds)

    loads["coords"].wait()
    left = points[pl.ds(0, dim), :].T
    left_sq = jnp.sum(left * left, axis=1, keepdims=True)

    def fill_block(slot, source):
        right = points[pl.ds(slot * dim, dim), :]
        right_sq = jnp.sum(right * right, axis=0, keepdims=True)
        inner = jnp.dot(
            left, right, precision=lax.Precision.HIGHEST, preferred_element_type=f32
        )
        block = jnp.exp(-kernel_scale * (left_sq + right_sq - 2.0 * inner))
        if source is not None:
            wanted = group * n + source
            hit = jnp.float32(0.0)
            for k in range(near_ref.shape[1]):
                listed = (near_ref[0, k] == wanted) & (near_ref[0, k] >= 0)
                hit = hit + listed.astype(f32)
            block = hit * block
        blocks[:, slot * leaf : (slot + 1) * leaf] = block.astype(bf16)

    def near_dot(rounds, first, last):
        return jnp.dot(
            blocks[:, first * leaf : last * leaf],
            wide[rounds, first * leaf : last * leaf, :],
            preferred_element_type=f32,
        )

    prepare(0)
    pl.semaphore_wait(barrier, 2 * n - 1)
    up_start(0)
    tag_start()
    near_start(points, 0, dim)
    near_start(wide.at[0], 1, leaf)
    tree_go(0, 0, own_sends)
    every = range(PARTS)
    for rounds in range(ITERS):
        stage = rounds + 1
        if rounds > 0:
            prepare(rounds)
            send(rounds)
        else:
            fill_block(0, None)
            loads["farclus"].wait()
            loads["cluscoup"].wait()
            map_clusters()
            loads["far"].wait()
            loads["coup"].wait()
            map_partners()
            near_relay(points, 0, dim, every)
        acc[...] = ridge * direction[...] + near_dot(rounds, 0, 1)
        near_relay(wide.at[rounds], stage, leaf, every[:EARLY])
        couple(rounds)
        near_relay(wide.at[rounds], stage, leaf, every[EARLY:])
        tree_lanes(rounds, range(4))
        near_first(wide.at[rounds], stage, leaf)
        if rounds == 0:
            loads["near"].wait()
            near_first(points, 0, dim)
            fill_block(1, mate)
            fill_block(2, across)
            near_second(points, 0, dim)
            near_finish(points, 0, dim)
        acc[...] += near_dot(rounds, 1, 3)
        tree_sides(rounds)
        if rounds == 0:
            fill_block(3, me - 2 + 4 * row)
            fill_block(4, me - 1 + 2 * core)
        near_second(wide.at[rounds], stage, leaf)
        tree_wait(rounds, last_waits)
        level_one = jnp.dot(partners[...], skel[rounds], preferred_element_type=f32)
        near_finish(wide.at[rounds], stage, leaf)
        acc[...] += near_dot(rounds, 3, 5)
        down_all(rounds).wait_recv()
        coupled = c_in[rounds].reshape(outs, rank)
        down = lax.dot_general(
            transfer_rows, coupled, (((1,), (1,)), ((), ())), preferred_element_type=f32
        )
        far_part = jnp.dot(
            basis_p[...], (level_one + down).astype(bf16), preferred_element_type=f32
        )
        residual = res_ref[...] - (acc[...] + far_part)
        res_ref[...] = residual
        rho_next = 1.0 / (2.0 * sigma_ratio - contraction)
        moved_on = rho_next * contraction * direction[...] + 2.0 * rho_next / spread * residual
        direction[...] = moved_on
        sol_ref[...] += moved_on
        contraction = rho_next

    near_drain(points, 0, dim)
    tag_all().wait_send()
    for rounds in range(ITERS):
        near_drain(wide.at[rounds], rounds + 1, leaf)
        tree_drain(rounds)
        up_all(rounds).wait_send()
        down_all(rounds).wait_send()


def fused_body(
    coords,
    right_side,
    leaf_perm,
    near_list,
    far_leaves,
    couplings,
    transfer,
    leaf_basis,
    cluster_of,
    far_clusters,
    cluster_couplings,
    ridge_weight,
):
    n = lax.axis_size("dev")
    leaf, dim = coords.shape
    outs = right_side.shape[1]
    rank = transfer.shape[1]
    clusters = cluster_couplings.shape[0]
    width = outs // n
    bf16, f32 = jnp.bfloat16, jnp.float32
    vmem = pl.BlockSpec(memory_space=pltpu.VMEM)
    smem = pl.BlockSpec(memory_space=pltpu.SMEM)
    hbm = pl.BlockSpec(memory_space=pltpu.HBM)
    sem = pltpu.SemaphoreType.DMA
    stages = ITERS + 1
    out = jax.ShapeDtypeStruct((leaf, outs), f32)
    return pl.pallas_call(
        functools.partial(fused_kernel, n),
        out_shape=(out, out),
        in_specs=[hbm, hbm, hbm, hbm, hbm, hbm, hbm, hbm, smem, hbm, hbm, hbm],
        out_specs=(vmem, vmem),
        scratch_shapes=[
            pltpu.VMEM((5 * dim, leaf), f32),
            pltpu.VMEM((ITERS, 5 * leaf, outs), bf16),
            pltpu.VMEM((leaf, 5 * leaf), bf16),
            pltpu.VMEM((ITERS, n * rank, outs), bf16),
            pltpu.VMEM((ITERS, n, width + 16, rank), bf16),
            pltpu.VMEM((ITERS, n, width + 16, rank), bf16),
            pltpu.VMEM((n, 16, rank), bf16),
            pltpu.VMEM((width, clusters * rank), bf16),
            pltpu.VMEM((clusters * rank, clusters * rank), bf16),
            pltpu.VMEM((rank, n * rank), bf16),
            pltpu.VMEM((ITERS, n, width, rank), bf16),
            pltpu.VMEM((ITERS, n, width, rank), bf16),
            pltpu.VMEM((leaf, rank), bf16),
            pltpu.VMEM((rank, leaf), bf16),
            pltpu.VMEM((leaf, outs), f32),
            pltpu.VMEM((leaf, outs), f32),
            pltpu.VMEM(leaf_perm.shape, jnp.int32),
            pltpu.VMEM(leaf_basis.shape, bf16),
            pltpu.VMEM(transfer.shape, bf16),
            pltpu.VMEM(couplings.shape, bf16),
            pltpu.VMEM(cluster_couplings.shape, bf16),
            pltpu.VMEM((1, 1), f32),
            pltpu.SMEM(near_list.shape, jnp.int32),
            pltpu.SMEM(far_leaves.shape, jnp.int32),
            pltpu.SMEM(far_clusters.shape, jnp.int32),
            sem((11,)),
            sem((stages, 5, PARTS)),
            sem((stages, 5, PARTS)),
            sem((ITERS, 15)),
            sem((ITERS, n)),
            sem((2 * ITERS + 1,)),
            sem((2 * ITERS + 1,)),
        ],
        compiler_params=pltpu.CompilerParams(
            collective_id=0, has_side_effects=True, vmem_limit_bytes=48 << 20
        ),
        name="fused_solve",
    )(
        coords.T,
        right_side,
        leaf_perm,
        near_list,
        far_leaves,
        couplings,
        transfer,
        leaf_basis,
        cluster_of,
        far_clusters,
        cluster_couplings,
        ridge_weight.reshape(1, 1),
    )


def solution(mesh):
    fits = mesh.shape["grp"] == 2 and mesh.shape["dev"] % 4 == 0
    placed = (
        P(("grp", "dev"), None),
        P(("grp", "dev"), None),
        P(("grp", "dev"), None),
        P(("grp", "dev"), None),
        P(("grp", "dev"), None),
        P(("grp", "dev"), None, None, None),
        P(("grp", "dev"), None, None),
        P(("grp", "dev"), None),
        P(("grp", "dev")),
        P("grp", None),
        P("grp", None, None, None),
        P(),
    )
    return jax.shard_map(
        fused_body if fits else body,
        mesh=mesh,
        in_specs=placed,
        out_specs=(P(("grp", "dev"), None), P(("grp", "dev"), None)),
        check_vma=False,
    )
```

```python
import functools

import jax
import jax.numpy as jnp
from jax import lax
from jax.experimental import pallas as pl
from jax.experimental.pallas import tpu as pltpu
from jax.sharding import PartitionSpec as P

MESH = pl.DeviceIdType.MESH
PARTS = 4
EARLY = 2

REACH = 2
FARREACH = 8
ITERS = 2


kernel_scale = 1.0 / 32.0
spectrum_gap = 0.5
spectrum_top = 8.0


def from_behind(shard, axis, by):
    devices = lax.axis_size(axis)
    pairs = [(i, i + by) for i in range(devices) if 0 <= i + by < devices]
    return lax.ppermute(shard, axis, pairs)


def kernel_block(left_points, right_points):
    inner_products = jnp.dot(
        left_points,
        right_points.T,
        precision=lax.Precision.HIGHEST,
        preferred_element_type=jnp.float32,
    )
    distance = (
        jnp.sum(left_points * left_points, axis=1)[:, None]
        + jnp.sum(right_points * right_points, axis=1)[None, :]
        - 2.0 * inner_products
    )
    return jnp.exp(-kernel_scale * distance).astype(jnp.bfloat16)


def body(
    coords,
    right_side,
    leaf_perm,
    near_list,
    far_leaves,
    couplings,
    transfer,
    leaf_basis,
    cluster_of,
    far_clusters,
    cluster_couplings,
    ridge_weight,
):
    dev_count = lax.axis_size("dev")
    group_index = lax.axis_index("grp")
    leaf_id = group_index * dev_count + lax.axis_index("dev")
    clusters_here = far_clusters.shape[0]
    local_cluster = cluster_of[0] - group_index * clusters_here
    ordering = leaf_perm[0]
    near_offsets = [offset for offset in range(-REACH, REACH + 1) if offset != 0]
    far_offsets = [offset for offset in range(-FARREACH, FARREACH + 1) if abs(offset) > REACH]
    neighbours = [from_behind(coords, "dev", -offset) for offset in near_offsets]
    near_flags = [
        jnp.any((near_list[0] == leaf_id + offset) & (near_list[0] >= 0)).astype(jnp.float32)
        for offset in near_offsets
    ]
    far_hits = jnp.stack(
        [far_leaves[0] == leaf_id + offset for offset in far_offsets], axis=1
    ).astype(jnp.bfloat16)
    own_block = kernel_block(coords, coords)
    near_blocks = [kernel_block(coords, neighbour_points) for neighbour_points in neighbours]
    cluster_slots = (jnp.arange(clusters_here) == local_cluster).astype(jnp.float32)

    def operate(direction):
        values = direction.astype(jnp.bfloat16)
        near_sum = jnp.dot(own_block, values, preferred_element_type=jnp.float32)
        for position in range(len(near_offsets)):
            remote = from_behind(values, "dev", -near_offsets[position])
            block_here = near_blocks[position]
            near_term = near_flags[position] * jnp.dot(
                block_here, remote, preferred_element_type=jnp.float32
            )
            near_sum = near_sum + near_term
        skeleton = lax.dot_general(
            leaf_basis,
            values[ordering],
            (((0,), (0,)), ((), ())),
            preferred_element_type=jnp.float32,
        ).astype(jnp.bfloat16)
        remote_skeletons = jnp.stack(
            [from_behind(skeleton, "dev", -offset) for offset in far_offsets]
        )
        chosen = jnp.einsum(
            "kj,jbo->kbo", far_hits, remote_skeletons, preferred_element_type=jnp.float32
        ).astype(jnp.bfloat16)
        level_one = jnp.einsum(
            "kab,kbo->ao", couplings[0], chosen, preferred_element_type=jnp.float32
        )
        uplift = lax.dot_general(
            transfer[0], skeleton, (((0,), (0,)), ((), ())), preferred_element_type=jnp.float32
        )
        contrib = cluster_slots[:, None, None] * uplift[None]
        column_sums = lax.psum_scatter(contrib, "dev", scatter_dimension=2, tiled=True).astype(
            jnp.bfloat16
        )
        every_column = lax.all_gather(column_sums, "grp", axis=0, tiled=True)
        picked = every_column[far_clusters]
        partial_coupled = jnp.einsum(
            "ckab,ckbo->cao", cluster_couplings, picked, preferred_element_type=jnp.float32
        ).astype(jnp.bfloat16)
        whole_columns = lax.all_gather(partial_coupled, "dev", axis=2, tiled=True)
        coupled = whole_columns[local_cluster]
        downward = jnp.dot(transfer[0], coupled, preferred_element_type=jnp.float32)
        tree_rows = jnp.dot(
            leaf_basis,
            (level_one + downward).astype(jnp.bfloat16),
            preferred_element_type=jnp.float32,
        )
        far_part = jnp.zeros_like(tree_rows).at[ordering].set(tree_rows)
        return ridge_weight * direction + (near_sum + far_part)

    bottom_edge = ridge_weight + spectrum_gap
    top_edge = ridge_weight + spectrum_top
    centre = (top_edge + bottom_edge) / 2.0
    spread = (top_edge - bottom_edge) / 2.0
    sigma_ratio = centre / spread
    contraction = 1.0 / sigma_ratio
    direction = right_side / centre
    solution = direction
    residual = right_side
    for rounds in range(ITERS):
        residual = residual - operate(direction)
        rho_next = 1.0 / (2.0 * sigma_ratio - contraction)
        direction = rho_next * contraction * direction + 2.0 * rho_next / spread * residual
        solution = solution + direction
        contraction = rho_next
    return (solution, residual)


def fused_kernel(
    n,
    coords_hbm,
    right_hbm,
    perm_hbm,
    near_hbm,
    far_hbm,
    coup_hbm,
    transfer_hbm,
    basis_hbm,
    cluster_hbm,
    farclus_hbm,
    cluscoup_hbm,
    ridge_hbm,
    sol_ref,
    res_ref,
    points,
    wide,
    blocks,
    skel,
    up_out,
    up_in,
    tag_in,
    sums_t,
    pair_map,
    partners,
    c_out,
    c_in,
    basis_p,
    basis_t,
    acc,
    direction,
    perm_ref,
    basis_ref,
    transfer_ref,
    coup_ref,
    cluscoup_ref,
    ridge_ref,
    cluster_ref,
    near_ref,
    far_ref,
    farclus_ref,
    load_sem,
    near_send,
    near_recv,
    tree_send,
    tree_recv,
    wide_send,
    wide_recv,
):
    f32, bf16 = jnp.float32, jnp.bfloat16
    group = lax.axis_index("grp")
    me = lax.axis_index("dev")
    other = 1 - group
    chip = lax.div(me, 2)
    core = lax.rem(me, 2)
    row = lax.rem(chip, 2)
    mate = chip * 2 + (1 - core)
    across = me + 2 - 4 * row
    across_mate = mate + 2 - 4 * row
    leaf, outs = right_hbm.shape
    dim = coords_hbm.shape[0]
    rank = transfer_hbm.shape[1]
    clusters = cluscoup_hbm.shape[0]
    planes = n // 4
    plane = lax.div(me, 4)
    slicers = n // 2
    width = outs // slicers
    tag_rows = 16
    slices = (row == 1) == (plane < planes // 2)
    my_slice = plane * 2 + core

    def slicer(j):
        side = jnp.where(lax.div(j, 2) < planes // 2, 2, 0)
        return lax.div(j, 2) * 4 + side + lax.rem(j, 2)

    has_z = ((row == 0) & (me >= 4)) | ((row == 1) & (me + 4 < n))
    sends_z = ((row == 0) & (me + 4 < n)) | ((row == 1) & (me >= 4))
    z_target = jnp.where(sends_z, me + 4 - 8 * row, me)

    barrier = pltpu.get_barrier_semaphore()
    for step in range(n):
        place = lax.rem(me + step, n)
        pl.semaphore_signal(
            barrier, inc=1, device_id={"grp": other, "dev": place}, device_id_type=MESH
        )
        if step > 0:
            pl.semaphore_signal(barrier, inc=1, device_id={"dev": place}, device_id_type=MESH)

    loads = {}
    for name, source, target in (
        ("perm", perm_hbm, perm_ref),
        ("cluster", cluster_hbm, cluster_ref),
        ("basis", basis_hbm, basis_ref),
        ("ridge", ridge_hbm, ridge_ref),
        ("right", right_hbm, res_ref),
        ("transfer", transfer_hbm, transfer_ref),
        ("coords", coords_hbm, points.at[pl.ds(0, dim)]),
        ("near", near_hbm, near_ref),
        ("far", far_hbm, far_ref),
        ("farclus", farclus_hbm, farclus_ref),
        ("cluscoup", cluscoup_hbm, cluscoup_ref),
        ("coup", coup_hbm, coup_ref),
    ):
        loads[name] = pltpu.make_async_copy(source, target, load_sem.at[len(loads)])
        loads[name].start()

    def near_copy(buf, stage, source, slot, target, size, part):
        piece = size // PARTS
        return pltpu.make_async_remote_copy(
            src_ref=buf.at[pl.ds(source * size + part * piece, piece)],
            dst_ref=buf.at[pl.ds(slot * size + part * piece, piece)],
            send_sem=near_send.at[stage, slot, part],
            recv_sem=near_recv.at[stage, slot, part],
            device_id={"dev": target},
            device_id_type=MESH,
        )

    def near_start(buf, stage, size):
        for part in range(PARTS):
            near_copy(buf, stage, 0, 2, across, size, part).start()
        for part in range(PARTS):
            near_copy(buf, stage, 0, 1, mate, size, part).start()

        @pl.when(jnp.logical_not(has_z))
        def _():
            buf[pl.ds(3 * size, size), :] = jnp.zeros((size, buf.shape[1]), buf.dtype)

        @pl.when(jnp.logical_not(has_z) & (core == row))
        def _():
            buf[pl.ds(4 * size, size), :] = jnp.zeros((size, buf.shape[1]), buf.dtype)

    def near_relay(buf, stage, size, parts):
        for part in parts:
            near_copy(buf, stage, 0, 2, across, size, part).wait_recv()

            @pl.when(sends_z)
            def _():
                near_copy(buf, stage, 2, 3, z_target, size, part).start()

            @pl.when(core == row)
            def _():
                near_copy(buf, stage, 2, 4, mate, size, part).start()

    def near_second(buf, stage, size):
        for part in range(PARTS):

            @pl.when(has_z)
            def _():
                near_copy(buf, stage, 2, 3, mate, size, part).wait_recv()

            @pl.when(has_z & (core != row))
            def _():
                near_copy(buf, stage, 3, 4, mate, size, part).start()

    def near_first(buf, stage, size):
        for part in range(PARTS):
            near_copy(buf, stage, 0, 1, mate, size, part).wait_recv()

    def near_finish(buf, stage, size):
        for part in range(PARTS):

            @pl.when(has_z | (core != row))
            def _():
                near_copy(buf, stage, 0, 4, mate, size, part).wait_recv()

    def near_drain(buf, stage, size):
        for part in range(PARTS):
            near_copy(buf, stage, 0, 1, mate, size, part).wait_send()
            near_copy(buf, stage, 0, 2, across, size, part).wait_send()

            @pl.when(sends_z)
            def _():
                near_copy(buf, stage, 2, 3, z_target, size, part).wait_send()

            @pl.when(has_z | (core == row))
            def _():
                near_copy(buf, stage, 0, 4, mate, size, part).wait_send()

    heading = 1 - 2 * row

    def inside(owner):
        return (owner >= 0) & (owner < n)

    def tree_copy(rounds, step, owner, target):
        owner = jnp.clip(owner, 0, n - 1)
        place = pl.ds(pl.multiple_of(owner * rank, 16), rank)
        return pltpu.make_async_remote_copy(
            src_ref=skel.at[rounds, place],
            dst_ref=skel.at[rounds, place],
            send_sem=tree_send.at[rounds, step],
            recv_sem=tree_recv.at[rounds, owner],
            device_id={"dev": jnp.clip(target, 0, n - 1)},
            device_id_type=MESH,
        )

    ahead, behind = me + 4 * heading, me - 4 * heading
    own_sends = [
        (inside(ahead), me, ahead),
        (inside(behind), me, behind),
        (inside(ahead + 4 * heading), me, ahead + 4 * heading),
        (inside(behind - 4 * heading), me, behind - 4 * heading),
        (core == row, me, across_mate),
    ]
    lanes = []
    for hops in (1, -1, -2, 2):
        owner = me - 4 * heading * hops
        here = inside(owner)
        if hops == 1:
            sends = [(here, mate), (here, across)]
        elif hops == -1:
            sends = [(here, mate), (here & (core != row), across_mate)]
        elif hops == -2:
            sends = [(here, across), (here & (core == row), mate)]
        else:
            sends = [(here & (core != row), mate)]
        lanes.append((here, owner, [(when, owner, target) for when, target in sends]))
    side_waits = [
        (inside(across + 4 * heading), across + 4 * heading),
        (inside(across - 8 * heading), across - 8 * heading),
    ]
    side_sends = [(here, owner, mate) for here, owner in side_waits]
    last_waits = [
        (core == row, across_mate),
        ((core == 1 - row) & inside(across_mate - 4 * heading), across_mate - 4 * heading),
        (inside(mate - 4), mate - 4),
        (inside(mate + 4), mate + 4),
        ((core == 0) & inside(mate - 8), mate - 8),
        ((core == 1) & inside(mate + 8), mate + 8),
        (inside(across_mate + 4 * heading), across_mate + 4 * heading),
        (inside(across_mate - 8 * heading), across_mate - 8 * heading),
    ]
    every_send = list(own_sends)
    lane_first = []
    for _, _, sends in lanes:
        lane_first.append(len(every_send))
        every_send += sends
    side_first = len(every_send)
    every_send += side_sends

    def tree_go(rounds, first, sends):
        for step, (when, owner, target) in enumerate(sends):

            @pl.when(when)
            def _():
                tree_copy(rounds, first + step, owner, target).start()

    def tree_wait(rounds, waits):
        for when, owner in waits:

            @pl.when(when)
            def _():
                tree_copy(rounds, 0, owner, mate).wait_recv()

    def tree_lanes(rounds, chosen):
        for lane in chosen:
            here, owner, sends = lanes[lane]
            tree_wait(rounds, [(here, owner)])
            tree_go(rounds, lane_first[lane], sends)

    def tree_sides(rounds):
        for side in range(2):
            tree_wait(rounds, side_waits[side : side + 1])
            tree_go(rounds, side_first + side, side_sends[side : side + 1])

    def tree_drain(rounds):
        for step, (when, owner, target) in enumerate(every_send):

            @pl.when(when)
            def _():
                tree_copy(rounds, step, owner, target).wait_send()

    def wide_copy(source, target, sem, device):
        return pltpu.make_async_remote_copy(
            src_ref=source,
            dst_ref=target,
            send_sem=wide_send.at[sem],
            recv_sem=wide_recv.at[sem],
            device_id=device,
            device_id_type=MESH,
        )

    def up_rows(rounds):
        return width + tag_rows if rounds == 0 else width

    def up_start(rounds):
        for step in range(slicers):
            j = lax.rem(my_slice + slicers // 2 + step, slicers)
            rows = pl.ds(0, up_rows(rounds))
            wide_copy(
                up_out.at[rounds, j, rows],
                up_in.at[rounds, me, rows],
                rounds,
                {"grp": other, "dev": slicer(j)},
            ).start()

    def up_all(rounds, count):
        whole = up_in.at[rounds, pl.ds(0, count), pl.ds(0, up_rows(rounds))]
        return wide_copy(whole, whole, rounds, {"grp": other})

    def tag_start():
        for step in range(slicers):
            place = slicer(lax.rem(my_slice + step, slicers))

            @pl.when(place != me)
            def _():
                wide_copy(tag_in.at[me], tag_in.at[me], ITERS, {"dev": place}).start()

    def tag_all(count):
        whole = tag_in.at[pl.ds(0, count)]
        return wide_copy(whole, whole, ITERS, {"dev": mate})

    def down_start(rounds):
        for step in range(1, n):
            place = lax.rem(me + step, n)
            wide_copy(
                c_out.at[rounds, place],
                c_in.at[rounds, my_slice],
                ITERS + 1 + rounds,
                {"dev": place},
            ).start()

    def down_all(rounds, count):
        whole = c_out.at[rounds, pl.ds(0, count)]
        return wide_copy(whole, whole, ITERS + 1 + rounds, {"dev": mate})

    loads["cluster"].wait()
    local_cluster = cluster_ref[0, 0] - group * clusters
    lane_rows = lax.broadcasted_iota(jnp.int32, (tag_rows, rank), 0)
    tags = jnp.where(lane_rows == local_cluster, 1.0, 0.0).astype(bf16)
    tag_in[me] = tags
    for place in range(slicers):
        up_out[0, place, width:, :] = tags

    loads["perm"].wait()
    targets = lax.broadcasted_iota(jnp.int32, (leaf, leaf), 0)
    one_hot = jnp.where(targets == perm_ref[...], 1.0, 0.0).astype(bf16)
    loads["basis"].wait()
    placed = jnp.dot(one_hot, basis_ref[...], preferred_element_type=f32)
    basis_p[...] = placed.astype(bf16)
    basis_t[...] = placed.T.astype(bf16)
    loads["ridge"].wait()
    ridge = ridge_ref[...]
    bottom_edge = ridge + spectrum_gap
    top_edge = ridge + spectrum_top
    centre = (top_edge + bottom_edge) / 2.0
    spread = (top_edge - bottom_edge) / 2.0
    sigma_ratio = centre / spread
    contraction = 1.0 / sigma_ratio
    loads["right"].wait()
    start = res_ref[...] / centre
    direction[...] = start
    sol_ref[...] = start
    loads["transfer"].wait()
    transfer_rows = transfer_ref[0]

    def prepare(rounds):
        values = direction[...].astype(bf16)
        wide[rounds, pl.ds(0, leaf), :] = values
        skeleton = jnp.dot(basis_t[...], values, preferred_element_type=f32)
        skel[rounds, pl.ds(pl.multiple_of(me * rank, 16), rank), :] = skeleton.astype(bf16)
        uplift = jnp.dot(
            skeleton.T.astype(bf16), transfer_rows, preferred_element_type=f32
        ).astype(bf16)
        for place in range(slicers):
            up_out[rounds, place, 0:width, :] = uplift[place * width : (place + 1) * width, :]

    def send(rounds):
        up_start(rounds)
        near_start(wide.at[rounds], rounds + 1, leaf)
        tree_go(rounds, 0, own_sends)

    def map_clusters():
        for c in range(clusters):
            for place in range(clusters):
                total = jnp.zeros((rank, rank), f32)
                for k in range(farclus_ref.shape[1]):
                    hit = (farclus_ref[c, k] == other * clusters + place).astype(f32)
                    total = total + hit * cluscoup_ref[c, k].astype(f32)
                pair_map[place * rank : (place + 1) * rank, c * rank : (c + 1) * rank] = (
                    total.T.astype(bf16)
                )

    def map_partners():
        for place in range(n):
            total = jnp.zeros((rank, rank), f32)
            for k in range(far_ref.shape[1]):
                hit = (far_ref[0, k] == group * n + place).astype(f32)
                total = total + hit * coup_ref[0, k].astype(f32)
            partners[:, place * rank : (place + 1) * rank] = total.astype(bf16)

            @pl.when((jnp.abs(me - place) <= REACH) | (jnp.abs(me - place) > FARREACH))
            def _():
                for rounds in range(ITERS):
                    if rounds > 0 :
                        skel[rounds, place * rank : (place + 1) * rank, :] = jnp.zeros(
                            (rank, outs), bf16
                        )

                @pl.when(me != place)
                def _():
                    skel[0, place * rank : (place + 1) * rank, :] = jnp.zeros((rank, outs), bf16)

    def couple(rounds):
        @pl.when(slices)
        def _():
            up_all(rounds, n).wait_recv()
            totals = [jnp.zeros((width, rank), f32) for _ in range(clusters)]
            for place in range(n):
                part = up_in[rounds, place, 0:width, :].astype(f32)
                tag = up_in[0, place, width:, :].astype(f32)
                totals = [totals[c] + tag[c : c + 1, :] * part for c in range(clusters)]
            for c in range(clusters):
                sums_t[:, c * rank : (c + 1) * rank] = totals[c].astype(bf16)
            coupled = jnp.dot(sums_t[...], pair_map[...], preferred_element_type=f32)
            coupled = coupled.astype(bf16).astype(f32)
            if rounds == 0:
                tag_all(n - 1).wait_recv()
            for place in range(n):
                tag = tag_in[place].astype(f32)
                pick = jnp.zeros((width, rank), f32)
                for c in range(clusters):
                    pick = pick + tag[c : c + 1, :] * coupled[:, c * rank : (c + 1) * rank]
                c_out[rounds, place] = pick.astype(bf16)
            c_in[rounds, my_slice] = c_out[rounds, me]
            down_start(rounds)

    loads["coords"].wait()
    left = points[pl.ds(0, dim), :].T
    left_sq = jnp.sum(left * left, axis=1, keepdims=True)

    def fill_block(slot, source):
        right = points[pl.ds(slot * dim, dim), :]
        right_sq = jnp.sum(right * right, axis=0, keepdims=True)
        inner = jnp.dot(
            left, right, precision=lax.Precision.HIGHEST, preferred_element_type=f32
        )
        block = jnp.exp(-kernel_scale * (left_sq + right_sq - 2.0 * inner))
        if source is not None:
            wanted = group * n + source
            hit = jnp.float32(0.0)
            for k in range(near_ref.shape[1]):
                listed = (near_ref[0, k] == wanted) & (near_ref[0, k] >= 0)
                hit = hit + listed.astype(f32)
            block = hit * block
        blocks[:, slot * leaf : (slot + 1) * leaf] = block.astype(bf16)

    def near_dot(rounds, first, last):
        return jnp.dot(
            blocks[:, first * leaf : last * leaf],
            wide[rounds, first * leaf : last * leaf, :],
            preferred_element_type=f32,
        )

    prepare(0)
    pl.semaphore_wait(barrier, 2 * n - 1)
    up_start(0)
    tag_start()
    near_start(points, 0, dim)
    near_start(wide.at[0], 1, leaf)
    tree_go(0, 0, own_sends)
    parts = range(PARTS)
    for rounds in range(ITERS):
        stage = rounds + 1
        field = wide.at[rounds]
        if rounds > 0:
            prepare(rounds)
            send(rounds)
            near_first(field, stage, leaf)
            acc[...] = ridge * direction[...] + near_dot(rounds, 0, 2)
            near_relay(field, stage, leaf, parts[:EARLY])
            tree_lanes(rounds, (0, 1))
            couple(rounds)
            near_relay(field, stage, leaf, parts[EARLY:])
            tree_lanes(rounds, (2, 3))
        else:
            fill_block(0, None)
            loads["near"].wait()
            near_first(points, 0, dim)
            fill_block(1, mate)
            loads["farclus"].wait()
            loads["cluscoup"].wait()
            map_clusters()
            loads["far"].wait()
            loads["coup"].wait()
            map_partners()
            near_relay(points, 0, dim, parts[:1])
            near_first(field, stage, leaf)
            acc[...] = ridge * direction[...] + near_dot(rounds, 0, 2)
            near_relay(points, 0, dim, parts[1:])
            tree_lanes(rounds, (0, 1))
            couple(rounds)
            fill_block(2, across)
            near_relay(field, stage, leaf, parts[:EARLY])
            tree_lanes(rounds, (2,))
            near_second(points, 0, dim)
            near_relay(field, stage, leaf, parts[EARLY:])
            fill_block(3, me - 2 + 4 * row)
            near_finish(points, 0, dim)
            fill_block(4, me - 1 + 2 * core)
            tree_lanes(rounds, (3,))
        acc[...] += near_dot(rounds, 2, 3)
        tree_sides(rounds)
        near_second(field, stage, leaf)
        acc[...] += near_dot(rounds, 3, 4)
        tree_wait(rounds, last_waits)
        level_one = jnp.dot(partners[...], skel[rounds], preferred_element_type=f32)
        near_finish(field, stage, leaf)
        acc[...] += near_dot(rounds, 4, 5)

        @pl.when(slices)
        def _():
            down_all(rounds, slicers - 1).wait_recv()

        @pl.when(jnp.logical_not(slices))
        def _():
            down_all(rounds, slicers).wait_recv()

        coupled = c_in[rounds].reshape(outs, rank)
        down = lax.dot_general(
            transfer_rows, coupled, (((1,), (1,)), ((), ())), preferred_element_type=f32
        )
        far_part = jnp.dot(
            basis_p[...], (level_one + down).astype(bf16), preferred_element_type=f32
        )
        residual = res_ref[...] - (acc[...] + far_part)
        res_ref[...] = residual
        rho_next = 1.0 / (2.0 * sigma_ratio - contraction)
        moved_on = rho_next * contraction * direction[...] + 2.0 * rho_next / spread * residual
        direction[...] = moved_on
        sol_ref[...] += moved_on
        contraction = rho_next

    near_drain(points, 0, dim)

    @pl.when(slices)
    def _():
        tag_all(slicers - 1).wait_send()
        for rounds in range(ITERS):
            down_all(rounds, n - 1).wait_send()

    @pl.when(jnp.logical_not(slices))
    def _():
        tag_all(slicers).wait_send()

    for rounds in range(ITERS):
        near_drain(wide.at[rounds], rounds + 1, leaf)
        tree_drain(rounds)
        up_all(rounds, slicers).wait_send()


def fused_body(
    coords,
    right_side,
    leaf_perm,
    near_list,
    far_leaves,
    couplings,
    transfer,
    leaf_basis,
    cluster_of,
    far_clusters,
    cluster_couplings,
    ridge_weight,
):
    n = lax.axis_size("dev")
    leaf, dim = coords.shape
    outs = right_side.shape[1]
    rank = transfer.shape[1]
    clusters = cluster_couplings.shape[0]
    slicers = n // 2
    width = outs // slicers
    bf16, f32 = jnp.bfloat16, jnp.float32
    vmem = pl.BlockSpec(memory_space=pltpu.VMEM)
    hbm = pl.BlockSpec(memory_space=pltpu.HBM)
    sem = pltpu.SemaphoreType.DMA
    stages = ITERS + 1

    def stay(array):
        return pltpu.with_memory_space_constraint(array, pltpu.HBM)

    out = jax.ShapeDtypeStruct((leaf, outs), f32)
    return pl.pallas_call(
        functools.partial(fused_kernel, n),
        out_shape=(out, out),
        in_specs=[hbm] * 12,
        out_specs=(vmem, vmem),
        scratch_shapes=[
            pltpu.VMEM((5 * dim, leaf), f32),
            pltpu.VMEM((ITERS, 5 * leaf, outs), bf16),
            pltpu.VMEM((leaf, 5 * leaf), bf16),
            pltpu.VMEM((ITERS, n * rank, outs), bf16),
            pltpu.VMEM((ITERS, slicers, width + 16, rank), bf16),
            pltpu.VMEM((ITERS, n, width + 16, rank), bf16),
            pltpu.VMEM((n, 16, rank), bf16),
            pltpu.VMEM((width, clusters * rank), bf16),
            pltpu.VMEM((clusters * rank, clusters * rank), bf16),
            pltpu.VMEM((rank, n * rank), bf16),
            pltpu.VMEM((ITERS, n, width, rank), bf16),
            pltpu.VMEM((ITERS, slicers, width, rank), bf16),
            pltpu.VMEM((leaf, rank), bf16),
            pltpu.VMEM((rank, leaf), bf16),
            pltpu.VMEM((leaf, outs), f32),
            pltpu.VMEM((leaf, outs), f32),
            pltpu.VMEM(leaf_perm.shape, jnp.int32),
            pltpu.VMEM(leaf_basis.shape, bf16),
            pltpu.VMEM(transfer.shape, bf16),
            pltpu.VMEM(couplings.shape, bf16),
            pltpu.VMEM(cluster_couplings.shape, bf16),
            pltpu.VMEM((1, 1), f32),
            pltpu.SMEM((1, 1), jnp.int32),
            pltpu.SMEM(near_list.shape, jnp.int32),
            pltpu.SMEM(far_leaves.shape, jnp.int32),
            pltpu.SMEM(far_clusters.shape, jnp.int32),
            sem((12,)),
            sem((stages, 5, PARTS)),
            sem((stages, 5, PARTS)),
            sem((ITERS, 14)),
            sem((ITERS, n)),
            sem((2 * ITERS + 1,)),
            sem((2 * ITERS + 1,)),
        ],
        compiler_params=pltpu.CompilerParams(
            collective_id=0, has_side_effects=True, vmem_limit_bytes=48 << 20
        ),
        name="fused_solve",
    )(
        stay(coords.T),
        stay(right_side),
        stay(leaf_perm),
        stay(near_list),
        stay(far_leaves),
        stay(couplings),
        stay(transfer),
        stay(leaf_basis),
        cluster_of.reshape(1, 1),
        stay(far_clusters),
        stay(cluster_couplings),
        ridge_weight.reshape(1, 1),
    )


def solution(mesh):
    fits = mesh.shape["grp"] == 2 and mesh.shape["dev"] % 4 == 0
    placed = (
        P(("grp", "dev"), None),
        P(("grp", "dev"), None),
        P(("grp", "dev"), None),
        P(("grp", "dev"), None),
        P(("grp", "dev"), None),
        P(("grp", "dev"), None, None, None),
        P(("grp", "dev"), None, None),
        P(("grp", "dev"), None),
        P(("grp", "dev")),
        P("grp", None),
        P("grp", None, None, None),
        P(),
    )
    return jax.shard_map(
        fused_body if fits else body,
        mesh=mesh,
        in_specs=placed,
        out_specs=(P(("grp", "dev"), None), P(("grp", "dev"), None)),
        check_vma=False,
    )
```

```python
import functools

import jax
import jax.numpy as jnp
from jax import lax
from jax.experimental import pallas as pl
from jax.experimental.pallas import tpu as pltpu
from jax.sharding import PartitionSpec as P

MESH = pl.DeviceIdType.MESH
PARTS = 4
EARLY = 2

REACH = 2
FARREACH = 8
ITERS = 2


kernel_scale = 1.0 / 32.0
spectrum_gap = 0.5
spectrum_top = 8.0


def from_behind(shard, axis, by):
    devices = lax.axis_size(axis)
    pairs = [(i, i + by) for i in range(devices) if 0 <= i + by < devices]
    return lax.ppermute(shard, axis, pairs)


def kernel_block(left_points, right_points):
    inner_products = jnp.dot(
        left_points,
        right_points.T,
        precision=lax.Precision.HIGHEST,
        preferred_element_type=jnp.float32,
    )
    distance = (
        jnp.sum(left_points * left_points, axis=1)[:, None]
        + jnp.sum(right_points * right_points, axis=1)[None, :]
        - 2.0 * inner_products
    )
    return jnp.exp(-kernel_scale * distance).astype(jnp.bfloat16)


def body(
    coords,
    right_side,
    leaf_perm,
    near_list,
    far_leaves,
    couplings,
    transfer,
    leaf_basis,
    cluster_of,
    far_clusters,
    cluster_couplings,
    ridge_weight,
):
    dev_count = lax.axis_size("dev")
    group_index = lax.axis_index("grp")
    leaf_id = group_index * dev_count + lax.axis_index("dev")
    clusters_here = far_clusters.shape[0]
    local_cluster = cluster_of[0] - group_index * clusters_here
    ordering = leaf_perm[0]
    near_offsets = [offset for offset in range(-REACH, REACH + 1) if offset != 0]
    far_offsets = [offset for offset in range(-FARREACH, FARREACH + 1) if abs(offset) > REACH]
    neighbours = [from_behind(coords, "dev", -offset) for offset in near_offsets]
    near_flags = [
        jnp.any((near_list[0] == leaf_id + offset) & (near_list[0] >= 0)).astype(jnp.float32)
        for offset in near_offsets
    ]
    far_hits = jnp.stack(
        [far_leaves[0] == leaf_id + offset for offset in far_offsets], axis=1
    ).astype(jnp.bfloat16)
    own_block = kernel_block(coords, coords)
    near_blocks = [kernel_block(coords, neighbour_points) for neighbour_points in neighbours]
    cluster_slots = (jnp.arange(clusters_here) == local_cluster).astype(jnp.float32)

    def operate(direction):
        values = direction.astype(jnp.bfloat16)
        near_sum = jnp.dot(own_block, values, preferred_element_type=jnp.float32)
        for position in range(len(near_offsets)):
            remote = from_behind(values, "dev", -near_offsets[position])
            block_here = near_blocks[position]
            near_term = near_flags[position] * jnp.dot(
                block_here, remote, preferred_element_type=jnp.float32
            )
            near_sum = near_sum + near_term
        skeleton = lax.dot_general(
            leaf_basis,
            values[ordering],
            (((0,), (0,)), ((), ())),
            preferred_element_type=jnp.float32,
        ).astype(jnp.bfloat16)
        remote_skeletons = jnp.stack(
            [from_behind(skeleton, "dev", -offset) for offset in far_offsets]
        )
        chosen = jnp.einsum(
            "kj,jbo->kbo", far_hits, remote_skeletons, preferred_element_type=jnp.float32
        ).astype(jnp.bfloat16)
        level_one = jnp.einsum(
            "kab,kbo->ao", couplings[0], chosen, preferred_element_type=jnp.float32
        )
        uplift = lax.dot_general(
            transfer[0], skeleton, (((0,), (0,)), ((), ())), preferred_element_type=jnp.float32
        )
        contrib = cluster_slots[:, None, None] * uplift[None]
        column_sums = lax.psum_scatter(contrib, "dev", scatter_dimension=2, tiled=True).astype(
            jnp.bfloat16
        )
        every_column = lax.all_gather(column_sums, "grp", axis=0, tiled=True)
        picked = every_column[far_clusters]
        partial_coupled = jnp.einsum(
            "ckab,ckbo->cao", cluster_couplings, picked, preferred_element_type=jnp.float32
        ).astype(jnp.bfloat16)
        whole_columns = lax.all_gather(partial_coupled, "dev", axis=2, tiled=True)
        coupled = whole_columns[local_cluster]
        downward = jnp.dot(transfer[0], coupled, preferred_element_type=jnp.float32)
        tree_rows = jnp.dot(
            leaf_basis,
            (level_one + downward).astype(jnp.bfloat16),
            preferred_element_type=jnp.float32,
        )
        far_part = jnp.zeros_like(tree_rows).at[ordering].set(tree_rows)
        return ridge_weight * direction + (near_sum + far_part)

    bottom_edge = ridge_weight + spectrum_gap
    top_edge = ridge_weight + spectrum_top
    centre = (top_edge + bottom_edge) / 2.0
    spread = (top_edge - bottom_edge) / 2.0
    sigma_ratio = centre / spread
    contraction = 1.0 / sigma_ratio
    direction = right_side / centre
    solution = direction
    residual = right_side
    for rounds in range(ITERS):
        residual = residual - operate(direction)
        rho_next = 1.0 / (2.0 * sigma_ratio - contraction)
        direction = rho_next * contraction * direction + 2.0 * rho_next / spread * residual
        solution = solution + direction
        contraction = rho_next
    return (solution, residual)


def interval(ridge):
    bottom_edge = ridge + spectrum_gap
    top_edge = ridge + spectrum_top
    centre = (top_edge + bottom_edge) / 2.0
    spread = (top_edge - bottom_edge) / 2.0
    return centre, spread, centre / spread


def momentum(sigma_ratio, spread, contraction):
    rho_next = 1.0 / (2.0 * sigma_ratio - contraction)
    return rho_next, rho_next * contraction, 2.0 * rho_next / spread


def fused_kernel(
    n,
    coords_hbm,
    right_hbm,
    perm_hbm,
    near_hbm,
    far_hbm,
    coup_hbm,
    transfer_hbm,
    basis_hbm,
    cluster_hbm,
    farclus_hbm,
    cluscoup_hbm,
    ridge_hbm,
    sol_ref,
    res_ref,
    acc,
    gain_ref,
    points,
    wide,
    blocks,
    skel,
    up_out,
    up_in,
    tag_in,
    up_tags,
    sums_t,
    pair_map,
    partners,
    c_out,
    c_in,
    basis_p,
    basis_t,
    left_parts,
    left_col,
    direction,
    perm_ref,
    basis_ref,
    transfer_ref,
    coup_ref,
    cluscoup_ref,
    ridge_ref,
    cluster_ref,
    near_ref,
    far_ref,
    farclus_ref,
    load_sem,
    near_send,
    near_recv,
    tree_send,
    tree_recv,
    wide_send,
    wide_recv,
):
    f32, bf16 = jnp.float32, jnp.bfloat16
    group = lax.axis_index("grp")
    me = lax.axis_index("dev")
    other = 1 - group
    chip = lax.div(me, 2)
    core = lax.rem(me, 2)
    row = lax.rem(chip, 2)
    mate = chip * 2 + (1 - core)
    across = me + 2 - 4 * row
    across_mate = mate + 2 - 4 * row
    leaf, outs = right_hbm.shape
    dim = coords_hbm.shape[0]
    rank = transfer_hbm.shape[1]
    clusters = cluscoup_hbm.shape[0]
    planes = n // 4
    plane = lax.div(me, 4)
    slicers = n // 2
    width = outs // slicers
    slices = (row == 1) == (plane < planes // 2)
    my_slice = plane * 2 + core

    def slicer(j):
        side = jnp.where(lax.div(j, 2) < planes // 2, 2, 0)
        return lax.div(j, 2) * 4 + side + lax.rem(j, 2)

    has_z = ((row == 0) & (me >= 4)) | ((row == 1) & (me + 4 < n))
    sends_z = ((row == 0) & (me + 4 < n)) | ((row == 1) & (me >= 4))
    z_target = jnp.where(sends_z, me + 4 - 8 * row, me)

    barrier = pltpu.get_barrier_semaphore()
    for step in range(n):
        place = lax.rem(me + step, n)
        pl.semaphore_signal(
            barrier, inc=1, device_id={"grp": other, "dev": place}, device_id_type=MESH
        )
        if step > 0:
            pl.semaphore_signal(barrier, inc=1, device_id={"dev": place}, device_id_type=MESH)

    loads = {}
    for name, source, target in (
        ("perm", perm_hbm, perm_ref),
        ("cluster", cluster_hbm, cluster_ref),
        ("basis", basis_hbm, basis_ref),
        ("ridge", ridge_hbm, ridge_ref),
        ("right", right_hbm, res_ref),
        ("transfer", transfer_hbm, transfer_ref),
        ("coords", coords_hbm, points.at[pl.ds(0, dim)]),
        ("near", near_hbm, near_ref),
        ("far", far_hbm, far_ref),
        ("farclus", farclus_hbm, farclus_ref),
        ("cluscoup", cluscoup_hbm, cluscoup_ref),
        ("coup", coup_hbm, coup_ref),
    ):
        loads[name] = pltpu.make_async_copy(source, target, load_sem.at[len(loads)])
        loads[name].start()

    def near_copy(buf, stage, source, slot, target, size, part):
        piece = size // PARTS
        return pltpu.make_async_remote_copy(
            src_ref=buf.at[pl.ds(source * size + part * piece, piece)],
            dst_ref=buf.at[pl.ds(slot * size + part * piece, piece)],
            send_sem=near_send.at[stage, slot, part],
            recv_sem=near_recv.at[stage, slot, part],
            device_id={"dev": target},
            device_id_type=MESH,
        )

    def near_start(buf, stage, size):
        for part in range(PARTS):
            near_copy(buf, stage, 0, 2, across, size, part).start()
        for part in range(PARTS):
            near_copy(buf, stage, 0, 1, mate, size, part).start()

        @pl.when(jnp.logical_not(has_z))
        def _():
            buf[pl.ds(3 * size, size), :] = jnp.zeros((size, buf.shape[1]), buf.dtype)

        @pl.when(jnp.logical_not(has_z) & (core == row))
        def _():
            buf[pl.ds(4 * size, size), :] = jnp.zeros((size, buf.shape[1]), buf.dtype)

    def near_relay(buf, stage, size, parts):
        for part in parts:
            near_copy(buf, stage, 0, 2, across, size, part).wait_recv()

            @pl.when(sends_z)
            def _():
                near_copy(buf, stage, 2, 3, z_target, size, part).start()

            @pl.when(core == row)
            def _():
                near_copy(buf, stage, 2, 4, mate, size, part).start()

    def near_second(buf, stage, size):
        for part in range(PARTS):

            @pl.when(has_z)
            def _():
                near_copy(buf, stage, 2, 3, mate, size, part).wait_recv()

            @pl.when(has_z & (core != row))
            def _():
                near_copy(buf, stage, 3, 4, mate, size, part).start()

    def near_first(buf, stage, size):
        for part in range(PARTS):
            near_copy(buf, stage, 0, 1, mate, size, part).wait_recv()

    def near_finish(buf, stage, size):
        for part in range(PARTS):

            @pl.when(has_z | (core != row))
            def _():
                near_copy(buf, stage, 0, 4, mate, size, part).wait_recv()

    def near_drain(buf, stage, size):
        for part in range(PARTS):
            near_copy(buf, stage, 0, 1, mate, size, part).wait_send()
            near_copy(buf, stage, 0, 2, across, size, part).wait_send()

            @pl.when(sends_z)
            def _():
                near_copy(buf, stage, 2, 3, z_target, size, part).wait_send()

            @pl.when(has_z | (core == row))
            def _():
                near_copy(buf, stage, 0, 4, mate, size, part).wait_send()

    heading = 1 - 2 * row

    def inside(owner):
        return (owner >= 0) & (owner < n)

    def tree_copy(rounds, step, owner, target):
        owner = jnp.clip(owner, 0, n - 1)
        place = pl.ds(pl.multiple_of(owner * rank, 16), rank)
        return pltpu.make_async_remote_copy(
            src_ref=skel.at[rounds, place],
            dst_ref=skel.at[rounds, place],
            send_sem=tree_send.at[rounds, step],
            recv_sem=tree_recv.at[rounds, owner],
            device_id={"dev": jnp.clip(target, 0, n - 1)},
            device_id_type=MESH,
        )

    ahead, behind = me + 4 * heading, me - 4 * heading
    own_sends = [
        (inside(ahead), me, ahead),
        (inside(behind), me, behind),
        (inside(ahead + 4 * heading), me, ahead + 4 * heading),
        (inside(behind - 4 * heading), me, behind - 4 * heading),
        (core == row, me, across_mate),
    ]
    lanes = []
    for hops in (1, -1, -2, 2):
        owner = me - 4 * heading * hops
        here = inside(owner)
        if hops == 1:
            sends = [(here, mate), (here, across)]
        elif hops == -1:
            sends = [(here, mate), (here & (core != row), across_mate)]
        elif hops == -2:
            sends = [(here, across), (here & (core == row), mate)]
        else:
            sends = [(here & (core != row), mate)]
        lanes.append((here, owner, [(when, owner, target) for when, target in sends]))
    side_waits = [
        (inside(across + 4 * heading), across + 4 * heading),
        (inside(across - 8 * heading), across - 8 * heading),
    ]
    side_sends = [(here, owner, mate) for here, owner in side_waits]
    last_waits = [
        (core == row, across_mate),
        ((core == 1 - row) & inside(across_mate - 4 * heading), across_mate - 4 * heading),
        (inside(mate - 4), mate - 4),
        (inside(mate + 4), mate + 4),
        ((core == 0) & inside(mate - 8), mate - 8),
        ((core == 1) & inside(mate + 8), mate + 8),
        (inside(across_mate + 4 * heading), across_mate + 4 * heading),
        (inside(across_mate - 8 * heading), across_mate - 8 * heading),
    ]
    every_send = list(own_sends)
    lane_first = []
    for _, _, sends in lanes:
        lane_first.append(len(every_send))
        every_send += sends
    side_first = len(every_send)
    every_send += side_sends

    def tree_go(rounds, first, sends):
        for step, (when, owner, target) in enumerate(sends):

            @pl.when(when)
            def _():
                tree_copy(rounds, first + step, owner, target).start()

    def tree_wait(rounds, waits):
        for when, owner in waits:

            @pl.when(when)
            def _():
                tree_copy(rounds, 0, owner, mate).wait_recv()

    def tree_lanes(rounds, chosen):
        for lane in chosen:
            here, owner, sends = lanes[lane]
            tree_wait(rounds, [(here, owner)])
            tree_go(rounds, lane_first[lane], sends)

    def tree_sides(rounds):
        for side in range(2):
            tree_wait(rounds, side_waits[side : side + 1])
            tree_go(rounds, side_first + side, side_sends[side : side + 1])

    def tree_drain(rounds):
        for step, (when, owner, target) in enumerate(every_send):

            @pl.when(when)
            def _():
                tree_copy(rounds, step, owner, target).wait_send()

    def wide_copy(source, target, sem, device):
        return pltpu.make_async_remote_copy(
            src_ref=source,
            dst_ref=target,
            send_sem=wide_send.at[sem],
            recv_sem=wide_recv.at[sem],
            device_id=device,
            device_id_type=MESH,
        )

    def up_start(rounds):
        for step in range(slicers):
            j = lax.rem(my_slice + slicers // 2 + step, slicers)
            wide_copy(
                up_out.at[rounds, j],
                up_in.at[rounds, me],
                rounds,
                {"grp": other, "dev": slicer(j)},
            ).start()

    def up_all(rounds, count):
        whole = up_in.at[rounds, pl.ds(0, count)]
        return wide_copy(whole, whole, rounds, {"grp": other})

    def tag_start():
        for step in range(slicers):
            place = slicer(lax.rem(my_slice + step, slicers))
            wide_copy(
                tag_in.at[0, me], tag_in.at[1, me], ITERS, {"grp": other, "dev": place}
            ).start()

            @pl.when(place != me)
            def _():
                wide_copy(tag_in.at[0, me], tag_in.at[0, me], ITERS, {"dev": place}).start()

    def tag_all(count):
        whole = up_tags.at[pl.ds(0, count)]
        return wide_copy(whole, whole, ITERS, {"dev": mate})

    def down_start(rounds):
        for step in range(1, n):
            place = lax.rem(me + step, n)
            wide_copy(
                c_out.at[rounds, place],
                c_in.at[rounds, my_slice],
                ITERS + 1 + rounds,
                {"dev": place},
            ).start()

    def down_all(rounds, count):
        whole = c_out.at[rounds, pl.ds(0, count)]
        return wide_copy(whole, whole, ITERS + 1 + rounds, {"dev": mate})

    loads["cluster"].wait()
    local_cluster = cluster_ref[0, 0] - group * clusters
    tag_in[0, me] = jnp.full((1, rank), local_cluster).astype(f32)

    loads["perm"].wait()
    targets = lax.broadcasted_iota(jnp.int32, (leaf, leaf), 0)
    one_hot = jnp.where(targets == perm_ref[...], 1.0, 0.0).astype(bf16)
    loads["basis"].wait()
    placed = jnp.dot(one_hot, basis_ref[...], preferred_element_type=f32)
    basis_p[...] = placed.astype(bf16)
    basis_t[...] = placed.T.astype(bf16)
    loads["ridge"].wait()
    ridge = ridge_ref[...]
    centre, spread, sigma_ratio = interval(ridge)
    contraction = 1.0 / sigma_ratio
    loads["right"].wait()
    start = res_ref[...] / centre
    direction[...] = start
    sol_ref[...] = start
    loads["transfer"].wait()
    transfer_rows = transfer_ref[0]

    def prepare(rounds):
        values = direction[...].astype(bf16)
        wide[rounds, pl.ds(0, leaf), :] = values
        skeleton = jnp.dot(basis_t[...], values, preferred_element_type=f32)
        skel[rounds, pl.ds(pl.multiple_of(me * rank, 16), rank), :] = skeleton.astype(bf16)
        uplift = jnp.dot(
            skeleton.T.astype(bf16), transfer_rows, preferred_element_type=f32
        ).astype(bf16)
        for place in range(slicers):
            up_out[rounds, place] = uplift[place * width : (place + 1) * width, :]

    def send(rounds):
        up_start(rounds)
        near_start(wide.at[rounds], rounds + 1, leaf)
        tree_go(rounds, 0, own_sends)

    def map_clusters():
        for c in range(clusters):
            for place in range(clusters):
                total = jnp.zeros((rank, rank), f32)
                for k in range(farclus_ref.shape[1]):
                    hit = (farclus_ref[c, k] == other * clusters + place).astype(f32)
                    total = total + hit * cluscoup_ref[c, k].astype(f32)
                pair_map[place * rank : (place + 1) * rank, c * rank : (c + 1) * rank] = (
                    total.T.astype(bf16)
                )

    def map_partners():
        for place in range(n):
            total = jnp.zeros((rank, rank), f32)
            for k in range(far_ref.shape[1]):
                hit = (far_ref[0, k] == group * n + place).astype(f32)
                total = total + hit * coup_ref[0, k].astype(f32)
            partners[:, place * rank : (place + 1) * rank] = total.astype(bf16)

            @pl.when((jnp.abs(me - place) <= REACH) | (jnp.abs(me - place) > FARREACH))
            def _():
                for rounds in range(ITERS):
                    if rounds > 0 :
                        skel[rounds, place * rank : (place + 1) * rank, :] = jnp.zeros(
                            (rank, outs), bf16
                        )

                @pl.when(me != place)
                def _():
                    skel[0, place * rank : (place + 1) * rank, :] = jnp.zeros((rank, outs), bf16)

    def couple(rounds):
        @pl.when(slices)
        def _():
            up_all(rounds, n).wait_recv()
            if rounds == 0:
                tag_all(2 * n - 1).wait_recv()
            totals = [jnp.zeros((width, rank), f32) for _ in range(clusters)]
            for place in range(n):
                part = up_in[rounds, place].astype(f32)
                for c in range(clusters):
                    mask = jnp.where(tag_in[1, place] == c, 1.0, 0.0)
                    totals[c] = totals[c] + mask * part
            for c in range(clusters):
                sums_t[:, c * rank : (c + 1) * rank] = totals[c].astype(bf16)
            coupled = jnp.dot(sums_t[...], pair_map[...], preferred_element_type=f32)
            for place in range(n):
                pick = jnp.zeros((width, rank), f32)
                for c in range(clusters):
                    mask = jnp.where(tag_in[0, place] == c, 1.0, 0.0)
                    pick = pick + mask * coupled[:, c * rank : (c + 1) * rank]
                c_out[rounds, place] = pick.astype(bf16)
            c_in[rounds, my_slice] = c_out[rounds, me]
            down_start(rounds)

    loads["coords"].wait()
    log2e = 1.4426950408889634

    def split(x):
        high = x.astype(bf16).astype(f32)
        middle = (x - high).astype(bf16).astype(f32)
        return high, middle, x - high - middle

    own = points[pl.ds(0, dim), :]
    high, middle, low = split(own * (2.0 * kernel_scale * log2e))
    left_parts[...] = (
        jnp.concatenate([high, high, middle, middle, high, low], axis=0).T.astype(bf16)
    )
    left_sq = jnp.sum(own * own, axis=0, keepdims=True) * (kernel_scale * log2e)
    left_col[...] = jnp.broadcast_to(left_sq, (128, leaf)).T

    def fill_block(slot, source):
        right = points[pl.ds(slot * dim, dim), :]
        lift = jnp.sum(right * right, axis=0, keepdims=True) * (kernel_scale * log2e)
        if source is not None:
            wanted = group * n + source
            hit = jnp.float32(0.0)
            for k in range(near_ref.shape[1]):
                listed = (near_ref[0, k] == wanted) & (near_ref[0, k] >= 0)
                hit = hit + listed.astype(f32)
            lift = lift + (1.0 - hit) * 1e4
        high, middle, low = split(right)
        right_parts = jnp.concatenate([high, middle, high, middle, low, high], axis=0)
        inner = jnp.dot(left_parts[...], right_parts.astype(bf16), preferred_element_type=f32)
        block = jnp.exp2(inner - (left_col[:, 0:1] + lift))
        blocks[:, slot * leaf : (slot + 1) * leaf] = block.astype(bf16)

    def near_dot(rounds, first, last):
        return jnp.dot(
            blocks[:, first * leaf : last * leaf],
            wide[rounds, first * leaf : last * leaf, :],
            preferred_element_type=f32,
        )

    prepare(0)
    pl.semaphore_wait(barrier, 2 * n - 1)
    up_start(0)
    tag_start()
    near_start(points, 0, dim)
    near_start(wide.at[0], 1, leaf)
    tree_go(0, 0, own_sends)
    parts = range(PARTS)
    for rounds in range(ITERS):
        stage = rounds + 1
        field = wide.at[rounds]
        if rounds > 0:
            prepare(rounds)
            send(rounds)
            near_first(field, stage, leaf)
            acc[...] = ridge * direction[...] + near_dot(rounds, 0, 2)
            near_relay(field, stage, leaf, parts[:EARLY])
            tree_lanes(rounds, (0, 1))
            couple(rounds)
            near_relay(field, stage, leaf, parts[EARLY:])
            tree_lanes(rounds, (2, 3))
        else:
            fill_block(0, None)
            loads["near"].wait()
            near_first(points, 0, dim)
            fill_block(1, mate)
            loads["farclus"].wait()
            loads["cluscoup"].wait()
            map_clusters()
            loads["far"].wait()
            loads["coup"].wait()
            map_partners()
            near_relay(points, 0, dim, parts[:1])
            near_first(field, stage, leaf)
            acc[...] = ridge * direction[...] + near_dot(rounds, 0, 2)
            near_relay(points, 0, dim, parts[1:])
            tree_lanes(rounds, (0, 1))
            couple(rounds)
            fill_block(2, across)
            near_relay(field, stage, leaf, parts[:EARLY])
            tree_lanes(rounds, (2,))
            near_second(points, 0, dim)
            near_relay(field, stage, leaf, parts[EARLY:])
            fill_block(3, me - 2 + 4 * row)
            near_finish(points, 0, dim)
            fill_block(4, me - 1 + 2 * core)
            tree_lanes(rounds, (3,))
        acc[...] += near_dot(rounds, 2, 3)
        if rounds == ITERS - 1:
            _, keep, gain = momentum(sigma_ratio, spread, contraction)
            gain_ref[...] = jnp.broadcast_to(gain, (1, outs))
            sol_ref[...] += keep * direction[...]
        tree_sides(rounds)
        near_second(field, stage, leaf)
        acc[...] += near_dot(rounds, 3, 4)
        tree_wait(rounds, last_waits)
        level_one = jnp.dot(partners[...], skel[rounds], preferred_element_type=f32)
        near_finish(field, stage, leaf)
        acc[...] += near_dot(rounds, 4, 5)

        @pl.when(slices)
        def _():
            down_all(rounds, slicers - 1).wait_recv()

        @pl.when(jnp.logical_not(slices))
        def _():
            down_all(rounds, slicers).wait_recv()

        coupled = c_in[rounds].reshape(outs, rank)
        down = lax.dot_general(
            transfer_rows, coupled, (((1,), (1,)), ((), ())), preferred_element_type=f32
        )
        far_part = jnp.dot(
            basis_p[...], (level_one + down).astype(bf16), preferred_element_type=f32
        )
        if rounds == ITERS - 1:
            acc[...] += far_part
            break
        residual = res_ref[...] - (acc[...] + far_part)
        res_ref[...] = residual
        rho_next, keep, gain = momentum(sigma_ratio, spread, contraction)
        moved_on = keep * direction[...] + gain * residual
        direction[...] = moved_on
        sol_ref[...] += moved_on
        contraction = rho_next

    near_drain(points, 0, dim)

    @pl.when(slices)
    def _():
        tag_all(2 * slicers - 1).wait_send()
        for rounds in range(ITERS):
            down_all(rounds, n - 1).wait_send()

    @pl.when(jnp.logical_not(slices))
    def _():
        tag_all(2 * slicers).wait_send()

    for rounds in range(ITERS):
        near_drain(wide.at[rounds], rounds + 1, leaf)
        tree_drain(rounds)
        up_all(rounds, slicers).wait_send()


def fused_body(
    coords,
    right_side,
    leaf_perm,
    near_list,
    far_leaves,
    couplings,
    transfer,
    leaf_basis,
    cluster_of,
    far_clusters,
    cluster_couplings,
    ridge_weight,
):
    n = lax.axis_size("dev")
    leaf, dim = coords.shape
    outs = right_side.shape[1]
    rank = transfer.shape[1]
    clusters = cluster_couplings.shape[0]
    slicers = n // 2
    width = outs // slicers
    bf16, f32 = jnp.bfloat16, jnp.float32
    vmem = pl.BlockSpec(memory_space=pltpu.VMEM)
    hbm = pl.BlockSpec(memory_space=pltpu.HBM)
    sem = pltpu.SemaphoreType.DMA
    stages = ITERS + 1

    def stay(array):
        return pltpu.with_memory_space_constraint(array, pltpu.HBM)

    out = jax.ShapeDtypeStruct((leaf, outs), f32)
    base, residual, applied, gain = pl.pallas_call(
        functools.partial(fused_kernel, n),
        out_shape=(out, out, out, jax.ShapeDtypeStruct((1, outs), f32)),
        in_specs=[hbm] * 12,
        out_specs=(vmem, vmem, vmem, vmem),
        scratch_shapes=[
            pltpu.VMEM((5 * dim, leaf), f32),
            pltpu.VMEM((ITERS, 5 * leaf, outs), bf16),
            pltpu.VMEM((leaf, 5 * leaf), bf16),
            pltpu.VMEM((ITERS, n * rank, outs), bf16),
            pltpu.VMEM((ITERS, slicers, width, rank), bf16),
            pltpu.VMEM((ITERS, n, width, rank), bf16),
            pltpu.VMEM((2, n, 1, rank), f32),
            pltpu.VMEM((2 * n, 1, rank), f32),
            pltpu.VMEM((width, clusters * rank), bf16),
            pltpu.VMEM((clusters * rank, clusters * rank), bf16),
            pltpu.VMEM((rank, n * rank), bf16),
            pltpu.VMEM((ITERS, n, width, rank), bf16),
            pltpu.VMEM((ITERS, slicers, width, rank), bf16),
            pltpu.VMEM((leaf, rank), bf16),
            pltpu.VMEM((rank, leaf), bf16),
            pltpu.VMEM((leaf, 6 * dim), bf16),
            pltpu.VMEM((leaf, 128), f32),
            pltpu.VMEM((leaf, outs), f32),
            pltpu.VMEM(leaf_perm.shape, jnp.int32),
            pltpu.VMEM(leaf_basis.shape, bf16),
            pltpu.VMEM(transfer.shape, bf16),
            pltpu.VMEM(couplings.shape, bf16),
            pltpu.VMEM(cluster_couplings.shape, bf16),
            pltpu.VMEM((1, 1), f32),
            pltpu.SMEM((1, 1), jnp.int32),
            pltpu.SMEM(near_list.shape, jnp.int32),
            pltpu.SMEM(far_leaves.shape, jnp.int32),
            pltpu.SMEM(far_clusters.shape, jnp.int32),
            sem((12,)),
            sem((stages, 5, PARTS)),
            sem((stages, 5, PARTS)),
            sem((ITERS, 14)),
            sem((ITERS, n)),
            sem((2 * ITERS + 1,)),
            sem((2 * ITERS + 1,)),
        ],
        compiler_params=pltpu.CompilerParams(
            collective_id=0, has_side_effects=True, vmem_limit_bytes=48 << 20
        ),
        name="fused_solve",
    )(
        stay(coords.T),
        stay(right_side),
        stay(leaf_perm),
        stay(near_list),
        stay(far_leaves),
        stay(couplings),
        stay(transfer),
        stay(leaf_basis),
        cluster_of.reshape(1, 1),
        stay(far_clusters),
        stay(cluster_couplings),
        ridge_weight.reshape(1, 1),
    )
    residual = residual - applied
    return base + gain * residual, residual


def solution(mesh):
    fits = mesh.shape["grp"] == 2 and mesh.shape["dev"] % 4 == 0
    placed = (
        P(("grp", "dev"), None),
        P(("grp", "dev"), None),
        P(("grp", "dev"), None),
        P(("grp", "dev"), None),
        P(("grp", "dev"), None),
        P(("grp", "dev"), None, None, None),
        P(("grp", "dev"), None, None),
        P(("grp", "dev"), None),
        P(("grp", "dev")),
        P("grp", None),
        P("grp", None, None, None),
        P(),
    )
    return jax.shard_map(
        fused_body if fits else body,
        mesh=mesh,
        in_specs=placed,
        out_specs=(P(("grp", "dev"), None), P(("grp", "dev"), None)),
        check_vma=False,
    )
```

```python
import functools

import jax
import jax.numpy as jnp
from jax import lax
from jax.experimental import pallas as pl
from jax.experimental.pallas import tpu as pltpu
from jax.sharding import PartitionSpec as P

MESH = pl.DeviceIdType.MESH
PARTS = 4
EARLY = 2

REACH = 2
FARREACH = 8
ITERS = 2


kernel_scale = 1.0 / 32.0
spectrum_gap = 0.5
spectrum_top = 8.0


def from_behind(shard, axis, by):
    devices = lax.axis_size(axis)
    pairs = [(i, i + by) for i in range(devices) if 0 <= i + by < devices]
    return lax.ppermute(shard, axis, pairs)


def kernel_block(left_points, right_points):
    inner_products = jnp.dot(
        left_points,
        right_points.T,
        precision=lax.Precision.HIGHEST,
        preferred_element_type=jnp.float32,
    )
    distance = (
        jnp.sum(left_points * left_points, axis=1)[:, None]
        + jnp.sum(right_points * right_points, axis=1)[None, :]
        - 2.0 * inner_products
    )
    return jnp.exp(-kernel_scale * distance).astype(jnp.bfloat16)


def body(
    coords,
    right_side,
    leaf_perm,
    near_list,
    far_leaves,
    couplings,
    transfer,
    leaf_basis,
    cluster_of,
    far_clusters,
    cluster_couplings,
    ridge_weight,
):
    dev_count = lax.axis_size("dev")
    group_index = lax.axis_index("grp")
    leaf_id = group_index * dev_count + lax.axis_index("dev")
    clusters_here = far_clusters.shape[0]
    local_cluster = cluster_of[0] - group_index * clusters_here
    ordering = leaf_perm[0]
    near_offsets = [offset for offset in range(-REACH, REACH + 1) if offset != 0]
    far_offsets = [offset for offset in range(-FARREACH, FARREACH + 1) if abs(offset) > REACH]
    neighbours = [from_behind(coords, "dev", -offset) for offset in near_offsets]
    near_flags = [
        jnp.any((near_list[0] == leaf_id + offset) & (near_list[0] >= 0)).astype(jnp.float32)
        for offset in near_offsets
    ]
    far_hits = jnp.stack(
        [far_leaves[0] == leaf_id + offset for offset in far_offsets], axis=1
    ).astype(jnp.bfloat16)
    own_block = kernel_block(coords, coords)
    near_blocks = [kernel_block(coords, neighbour_points) for neighbour_points in neighbours]
    cluster_slots = (jnp.arange(clusters_here) == local_cluster).astype(jnp.float32)

    def operate(direction):
        values = direction.astype(jnp.bfloat16)
        near_sum = jnp.dot(own_block, values, preferred_element_type=jnp.float32)
        for position in range(len(near_offsets)):
            remote = from_behind(values, "dev", -near_offsets[position])
            block_here = near_blocks[position]
            near_term = near_flags[position] * jnp.dot(
                block_here, remote, preferred_element_type=jnp.float32
            )
            near_sum = near_sum + near_term
        skeleton = lax.dot_general(
            leaf_basis,
            values[ordering],
            (((0,), (0,)), ((), ())),
            preferred_element_type=jnp.float32,
        ).astype(jnp.bfloat16)
        remote_skeletons = jnp.stack(
            [from_behind(skeleton, "dev", -offset) for offset in far_offsets]
        )
        chosen = jnp.einsum(
            "kj,jbo->kbo", far_hits, remote_skeletons, preferred_element_type=jnp.float32
        ).astype(jnp.bfloat16)
        level_one = jnp.einsum(
            "kab,kbo->ao", couplings[0], chosen, preferred_element_type=jnp.float32
        )
        uplift = lax.dot_general(
            transfer[0], skeleton, (((0,), (0,)), ((), ())), preferred_element_type=jnp.float32
        )
        contrib = cluster_slots[:, None, None] * uplift[None]
        column_sums = lax.psum_scatter(contrib, "dev", scatter_dimension=2, tiled=True).astype(
            jnp.bfloat16
        )
        every_column = lax.all_gather(column_sums, "grp", axis=0, tiled=True)
        picked = every_column[far_clusters]
        partial_coupled = jnp.einsum(
            "ckab,ckbo->cao", cluster_couplings, picked, preferred_element_type=jnp.float32
        ).astype(jnp.bfloat16)
        whole_columns = lax.all_gather(partial_coupled, "dev", axis=2, tiled=True)
        coupled = whole_columns[local_cluster]
        downward = jnp.dot(transfer[0], coupled, preferred_element_type=jnp.float32)
        tree_rows = jnp.dot(
            leaf_basis,
            (level_one + downward).astype(jnp.bfloat16),
            preferred_element_type=jnp.float32,
        )
        far_part = jnp.zeros_like(tree_rows).at[ordering].set(tree_rows)
        return ridge_weight * direction + (near_sum + far_part)

    bottom_edge = ridge_weight + spectrum_gap
    top_edge = ridge_weight + spectrum_top
    centre = (top_edge + bottom_edge) / 2.0
    spread = (top_edge - bottom_edge) / 2.0
    sigma_ratio = centre / spread
    contraction = 1.0 / sigma_ratio
    direction = right_side / centre
    solution = direction
    residual = right_side
    for rounds in range(ITERS):
        residual = residual - operate(direction)
        rho_next = 1.0 / (2.0 * sigma_ratio - contraction)
        direction = rho_next * contraction * direction + 2.0 * rho_next / spread * residual
        solution = solution + direction
        contraction = rho_next
    return (solution, residual)


def interval(ridge):
    bottom_edge = ridge + spectrum_gap
    top_edge = ridge + spectrum_top
    centre = (top_edge + bottom_edge) / 2.0
    spread = (top_edge - bottom_edge) / 2.0
    return centre, spread, centre / spread


def momentum(sigma_ratio, spread, contraction):
    rho_next = 1.0 / (2.0 * sigma_ratio - contraction)
    return rho_next, rho_next * contraction, 2.0 * rho_next / spread


def fused_kernel(
    n,
    coords_hbm,
    right_hbm,
    perm_hbm,
    near_hbm,
    far_hbm,
    coup_hbm,
    transfer_hbm,
    basis_hbm,
    cluster_hbm,
    farclus_hbm,
    cluscoup_hbm,
    ridge_hbm,
    sol_ref,
    res_ref,
    acc,
    gain_ref,
    points,
    wide,
    blocks,
    skel,
    up_out,
    up_in,
    tag_in,
    up_tags,
    sums_t,
    pair_map,
    partners,
    c_out,
    c_in,
    basis_p,
    basis_t,
    left_parts,
    left_col,
    direction,
    perm_ref,
    basis_ref,
    transfer_ref,
    coup_ref,
    cluscoup_ref,
    ridge_ref,
    cluster_ref,
    near_ref,
    far_ref,
    farclus_ref,
    load_sem,
    near_send,
    near_recv,
    tree_send,
    tree_recv,
    wide_send,
    wide_recv,
):
    f32, bf16 = jnp.float32, jnp.bfloat16
    group = lax.axis_index("grp")
    me = lax.axis_index("dev")
    other = 1 - group
    chip = lax.div(me, 2)
    core = lax.rem(me, 2)
    row = lax.rem(chip, 2)
    mate = chip * 2 + (1 - core)
    across = me + 2 - 4 * row
    across_mate = mate + 2 - 4 * row
    leaf, outs = right_hbm.shape
    dim = coords_hbm.shape[0]
    rank = transfer_hbm.shape[1]
    clusters = cluscoup_hbm.shape[0]
    planes = n // 4
    plane = lax.div(me, 4)
    slicers = n // 2
    width = outs // slicers
    slices = (row == 1) == (plane < planes // 2)
    my_slice = plane * 2 + core

    def slicer(j):
        side = jnp.where(lax.div(j, 2) < planes // 2, 2, 0)
        return lax.div(j, 2) * 4 + side + lax.rem(j, 2)

    has_z = ((row == 0) & (me >= 4)) | ((row == 1) & (me + 4 < n))
    sends_z = ((row == 0) & (me + 4 < n)) | ((row == 1) & (me >= 4))
    z_target = jnp.where(sends_z, me + 4 - 8 * row, me)

    barrier = pltpu.get_barrier_semaphore()
    for step in range(n):
        place = lax.rem(me + step, n)
        pl.semaphore_signal(
            barrier, inc=1, device_id={"grp": other, "dev": place}, device_id_type=MESH
        )
        if step > 0:
            pl.semaphore_signal(barrier, inc=1, device_id={"dev": place}, device_id_type=MESH)

    loads = {}
    for name, source, target in (
        ("perm", perm_hbm, perm_ref),
        ("cluster", cluster_hbm, cluster_ref),
        ("basis", basis_hbm, basis_ref),
        ("ridge", ridge_hbm, ridge_ref),
        ("right", right_hbm, res_ref),
        ("transfer", transfer_hbm, transfer_ref),
        ("coords", coords_hbm, points.at[pl.ds(0, dim)]),
        ("near", near_hbm, near_ref),
        ("far", far_hbm, far_ref),
        ("farclus", farclus_hbm, farclus_ref),
        ("cluscoup", cluscoup_hbm, cluscoup_ref),
        ("coup", coup_hbm, coup_ref),
    ):
        loads[name] = pltpu.make_async_copy(source, target, load_sem.at[len(loads)])
        loads[name].start()

    def near_copy(buf, stage, source, slot, target, size, part):
        piece = size // PARTS
        return pltpu.make_async_remote_copy(
            src_ref=buf.at[pl.ds(source * size + part * piece, piece)],
            dst_ref=buf.at[pl.ds(slot * size + part * piece, piece)],
            send_sem=near_send.at[stage, slot, part],
            recv_sem=near_recv.at[stage, slot, part],
            device_id={"dev": target},
            device_id_type=MESH,
        )

    def near_start(buf, stage, size):
        for part in range(PARTS):
            near_copy(buf, stage, 0, 2, across, size, part).start()
        for part in range(PARTS):
            near_copy(buf, stage, 0, 1, mate, size, part).start()

        @pl.when(jnp.logical_not(has_z))
        def _():
            buf[pl.ds(3 * size, size), :] = jnp.zeros((size, buf.shape[1]), buf.dtype)

        @pl.when(jnp.logical_not(has_z) & (core == row))
        def _():
            buf[pl.ds(4 * size, size), :] = jnp.zeros((size, buf.shape[1]), buf.dtype)

    def near_relay(buf, stage, size, parts):
        for part in parts:
            near_copy(buf, stage, 0, 2, across, size, part).wait_recv()

            @pl.when(sends_z)
            def _():
                near_copy(buf, stage, 2, 3, z_target, size, part).start()

            @pl.when(core == row)
            def _():
                near_copy(buf, stage, 2, 4, mate, size, part).start()

    def near_second(buf, stage, size):
        for part in range(PARTS):

            @pl.when(has_z)
            def _():
                near_copy(buf, stage, 2, 3, mate, size, part).wait_recv()

            @pl.when(has_z & (core != row))
            def _():
                near_copy(buf, stage, 3, 4, mate, size, part).start()

    def near_first(buf, stage, size):
        for part in range(PARTS):
            near_copy(buf, stage, 0, 1, mate, size, part).wait_recv()

    def near_finish(buf, stage, size):
        for part in range(PARTS):

            @pl.when(has_z | (core != row))
            def _():
                near_copy(buf, stage, 0, 4, mate, size, part).wait_recv()

    def near_drain(buf, stage, size):
        for part in range(PARTS):
            near_copy(buf, stage, 0, 1, mate, size, part).wait_send()
            near_copy(buf, stage, 0, 2, across, size, part).wait_send()

            @pl.when(sends_z)
            def _():
                near_copy(buf, stage, 2, 3, z_target, size, part).wait_send()

            @pl.when(has_z | (core == row))
            def _():
                near_copy(buf, stage, 0, 4, mate, size, part).wait_send()

    heading = 1 - 2 * row

    def inside(owner):
        return (owner >= 0) & (owner < n)

    def tree_copy(rounds, step, owner, target):
        owner = jnp.clip(owner, 0, n - 1)
        place = pl.ds(pl.multiple_of(owner * rank, 16), rank)
        return pltpu.make_async_remote_copy(
            src_ref=skel.at[rounds, place],
            dst_ref=skel.at[rounds, place],
            send_sem=tree_send.at[rounds, step],
            recv_sem=tree_recv.at[rounds, owner],
            device_id={"dev": jnp.clip(target, 0, n - 1)},
            device_id_type=MESH,
        )

    ahead, behind = me + 4 * heading, me - 4 * heading
    own_sends = [
        (inside(ahead), me, ahead),
        (inside(behind), me, behind),
        (inside(ahead + 4 * heading), me, ahead + 4 * heading),
        (inside(behind - 4 * heading), me, behind - 4 * heading),
        (core == row, me, across_mate),
    ]
    lanes = []
    for hops in (1, -1, -2, 2):
        owner = me - 4 * heading * hops
        here = inside(owner)
        if hops == 1:
            sends = [(here, mate), (here, across)]
        elif hops == -1:
            sends = [(here, mate), (here & (core != row), across_mate)]
        elif hops == -2:
            sends = [(here, across), (here & (core == row), mate)]
        else:
            sends = [(here & (core != row), mate)]
        lanes.append((here, owner, [(when, owner, target) for when, target in sends]))
    side_waits = [
        (inside(across + 4 * heading), across + 4 * heading),
        (inside(across - 8 * heading), across - 8 * heading),
    ]
    side_sends = [(here, owner, mate) for here, owner in side_waits]
    last_waits = [
        (core == row, across_mate),
        ((core == 1 - row) & inside(across_mate - 4 * heading), across_mate - 4 * heading),
        (inside(mate - 4), mate - 4),
        (inside(mate + 4), mate + 4),
        ((core == 0) & inside(mate - 8), mate - 8),
        ((core == 1) & inside(mate + 8), mate + 8),
        (inside(across_mate + 4 * heading), across_mate + 4 * heading),
        (inside(across_mate - 8 * heading), across_mate - 8 * heading),
    ]
    every_send = list(own_sends)
    lane_first = []
    for _, _, sends in lanes:
        lane_first.append(len(every_send))
        every_send += sends
    side_first = len(every_send)
    every_send += side_sends

    def tree_go(rounds, first, sends):
        for step, (when, owner, target) in enumerate(sends):

            @pl.when(when)
            def _():
                tree_copy(rounds, first + step, owner, target).start()

    def tree_wait(rounds, waits):
        for when, owner in waits:

            @pl.when(when)
            def _():
                tree_copy(rounds, 0, owner, mate).wait_recv()

    def tree_lanes(rounds, chosen):
        for lane in chosen:
            here, owner, sends = lanes[lane]
            tree_wait(rounds, [(here, owner)])
            tree_go(rounds, lane_first[lane], sends)

    def tree_sides(rounds):
        for side in range(2):
            tree_wait(rounds, side_waits[side : side + 1])
            tree_go(rounds, side_first + side, side_sends[side : side + 1])

    def tree_drain(rounds):
        for step, (when, owner, target) in enumerate(every_send):

            @pl.when(when)
            def _():
                tree_copy(rounds, step, owner, target).wait_send()

    def wide_copy(source, target, sem, device):
        return pltpu.make_async_remote_copy(
            src_ref=source,
            dst_ref=target,
            send_sem=wide_send.at[sem],
            recv_sem=wide_recv.at[sem],
            device_id=device,
            device_id_type=MESH,
        )

    def up_start(rounds):
        for step in range(slicers):
            j = lax.rem(my_slice + slicers // 2 + step, slicers)
            wide_copy(
                up_out.at[rounds, j],
                up_in.at[rounds, me],
                rounds,
                {"grp": other, "dev": slicer(j)},
            ).start()

    def up_all(rounds, count):
        whole = up_in.at[rounds, pl.ds(0, count)]
        return wide_copy(whole, whole, rounds, {"grp": other})

    def tag_start():
        for step in range(slicers):
            place = slicer(lax.rem(my_slice + step, slicers))
            wide_copy(
                tag_in.at[0, me], tag_in.at[1, me], ITERS, {"grp": other, "dev": place}
            ).start()

            @pl.when(place != me)
            def _():
                wide_copy(tag_in.at[0, me], tag_in.at[0, me], ITERS, {"dev": place}).start()

    def tag_all(count):
        whole = up_tags.at[pl.ds(0, count)]
        return wide_copy(whole, whole, ITERS, {"dev": mate})

    def down_start(rounds):
        for step in range(1, n):
            place = lax.rem(me + step, n)
            wide_copy(
                c_out.at[rounds, place],
                c_in.at[rounds, my_slice],
                ITERS + 1 + rounds,
                {"dev": place},
            ).start()

    def down_all(rounds, count):
        whole = c_out.at[rounds, pl.ds(0, count)]
        return wide_copy(whole, whole, ITERS + 1 + rounds, {"dev": mate})

    loads["cluster"].wait()
    local_cluster = cluster_ref[0, 0] - group * clusters
    tag_in[0, me] = jnp.full((1, rank), local_cluster).astype(f32)

    loads["perm"].wait()
    targets = lax.broadcasted_iota(jnp.int32, (leaf, leaf), 0)
    one_hot = jnp.where(targets == perm_ref[...], 1.0, 0.0).astype(bf16)
    loads["basis"].wait()
    placed = jnp.dot(one_hot, basis_ref[...], preferred_element_type=f32)
    basis_p[...] = placed.astype(bf16)
    basis_t[...] = placed.T.astype(bf16)
    loads["ridge"].wait()
    ridge = ridge_ref[...]
    centre, spread, sigma_ratio = interval(ridge)
    contraction = 1.0 / sigma_ratio
    loads["right"].wait()
    start = res_ref[...] / centre
    direction[...] = start
    sol_ref[...] = start
    loads["transfer"].wait()
    transfer_rows = transfer_ref[0]

    def prepare(rounds):
        values = direction[...].astype(bf16)
        wide[rounds, pl.ds(0, leaf), :] = values
        skeleton = jnp.dot(basis_t[...], values, preferred_element_type=f32)
        skel[rounds, pl.ds(pl.multiple_of(me * rank, 16), rank), :] = skeleton.astype(bf16)
        uplift = jnp.dot(
            skeleton.T.astype(bf16), transfer_rows, preferred_element_type=f32
        ).astype(bf16)
        for place in range(slicers):
            up_out[rounds, place] = uplift[place * width : (place + 1) * width, :]

    def send(rounds):
        up_start(rounds)
        near_start(wide.at[rounds], rounds + 1, leaf)
        tree_go(rounds, 0, own_sends)

    def map_clusters():
        for c in range(clusters):
            for place in range(clusters):
                total = jnp.zeros((rank, rank), f32)
                for k in range(farclus_ref.shape[1]):
                    hit = (farclus_ref[c, k] == other * clusters + place).astype(f32)
                    total = total + hit * cluscoup_ref[c, k].astype(f32)
                pair_map[place * rank : (place + 1) * rank, c * rank : (c + 1) * rank] = (
                    total.T.astype(bf16)
                )

    def map_partners():
        for place in range(n):
            total = jnp.zeros((rank, rank), f32)
            for k in range(far_ref.shape[1]):
                hit = (far_ref[0, k] == group * n + place).astype(f32)
                total = total + hit * coup_ref[0, k].astype(f32)
            partners[:, place * rank : (place + 1) * rank] = total.astype(bf16)

            @pl.when((jnp.abs(me - place) <= REACH) | (jnp.abs(me - place) > FARREACH))
            def _():
                for rounds in range(ITERS):
                    if rounds > 0 :
                        skel[rounds, place * rank : (place + 1) * rank, :] = jnp.zeros(
                            (rank, outs), bf16
                        )

                @pl.when(me != place)
                def _():
                    skel[0, place * rank : (place + 1) * rank, :] = jnp.zeros((rank, outs), bf16)

    def couple(rounds):
        @pl.when(slices)
        def _():
            up_all(rounds, n).wait_recv()
            if rounds == 0:
                tag_all(2 * n - 1).wait_recv()
            totals = [jnp.zeros((width, rank), f32) for _ in range(clusters)]
            for place in range(n):
                part = up_in[rounds, place].astype(f32)
                for c in range(clusters):
                    mask = jnp.where(tag_in[1, place] == c, 1.0, 0.0)
                    totals[c] = totals[c] + mask * part
            for c in range(clusters):
                sums_t[:, c * rank : (c + 1) * rank] = totals[c].astype(bf16)
            coupled = jnp.dot(sums_t[...], pair_map[...], preferred_element_type=f32)
            for place in range(n):
                pick = jnp.zeros((width, rank), f32)
                for c in range(clusters):
                    mask = jnp.where(tag_in[0, place] == c, 1.0, 0.0)
                    pick = pick + mask * coupled[:, c * rank : (c + 1) * rank]
                c_out[rounds, place] = pick.astype(bf16)
            c_in[rounds, my_slice] = c_out[rounds, me]
            down_start(rounds)

    loads["coords"].wait()
    log2e = 1.4426950408889634

    def split(x):
        high = x.astype(bf16).astype(f32)
        middle = (x - high).astype(bf16).astype(f32)
        return high, middle, x - high - middle

    own = points[pl.ds(0, dim), :]
    high, middle, low = split(own * (2.0 * kernel_scale * log2e))
    left_parts[...] = (
        jnp.concatenate([high, high, middle, middle, high, low], axis=0).T.astype(bf16)
    )
    left_sq = jnp.sum(own * own, axis=0, keepdims=True) * (kernel_scale * log2e)
    left_col[...] = jnp.broadcast_to(left_sq, (128, leaf)).T

    def fill_block(slot, source):
        right = points[pl.ds(slot * dim, dim), :]
        lift = jnp.sum(right * right, axis=0, keepdims=True) * (kernel_scale * log2e)
        if source is not None:
            wanted = group * n + source
            hit = jnp.float32(0.0)
            for k in range(near_ref.shape[1]):
                listed = (near_ref[0, k] == wanted) & (near_ref[0, k] >= 0)
                hit = hit + listed.astype(f32)
            lift = lift + (1.0 - hit) * 1e4
        high, middle, low = split(right)
        right_parts = jnp.concatenate([high, middle, high, middle, low, high], axis=0)
        inner = jnp.dot(left_parts[...], right_parts.astype(bf16), preferred_element_type=f32)
        block = jnp.exp2(inner - (left_col[:, 0:1] + lift))
        blocks[:, slot * leaf : (slot + 1) * leaf] = block.astype(bf16)

    def near_dot(rounds, first, last):
        return jnp.dot(
            blocks[:, first * leaf : last * leaf],
            wide[rounds, first * leaf : last * leaf, :],
            preferred_element_type=f32,
        )

    prepare(0)
    pl.semaphore_wait(barrier, 2 * n - 1)
    up_start(0)
    tag_start()
    near_start(points, 0, dim)
    near_start(wide.at[0], 1, leaf)
    tree_go(0, 0, own_sends)
    parts = range(PARTS)
    for rounds in range(ITERS):
        stage = rounds + 1
        field = wide.at[rounds]
        if rounds > 0:
            prepare(rounds)
            send(rounds)
            near_first(field, stage, leaf)
            acc[...] = ridge * direction[...] + near_dot(rounds, 0, 2)
            near_relay(field, stage, leaf, parts[:EARLY])
            tree_lanes(rounds, (0, 1))
            couple(rounds)
            near_relay(field, stage, leaf, parts[EARLY:])
            tree_lanes(rounds, (2, 3))
        else:
            fill_block(0, None)
            loads["near"].wait()
            near_first(points, 0, dim)
            fill_block(1, mate)
            loads["farclus"].wait()
            loads["cluscoup"].wait()
            map_clusters()
            loads["far"].wait()
            loads["coup"].wait()
            map_partners()
            near_relay(points, 0, dim, parts[:1])
            near_first(field, stage, leaf)
            acc[...] = ridge * direction[...] + near_dot(rounds, 0, 2)
            near_relay(points, 0, dim, parts[1:])
            tree_lanes(rounds, (0, 1))
            couple(rounds)
            fill_block(2, across)
            near_relay(field, stage, leaf, parts[:EARLY])
            tree_lanes(rounds, (2,))
            near_second(points, 0, dim)
            near_relay(field, stage, leaf, parts[EARLY:])
            fill_block(3, me - 2 + 4 * row)
            near_finish(points, 0, dim)
            fill_block(4, me - 1 + 2 * core)
            tree_lanes(rounds, (3,))
        acc[...] += near_dot(rounds, 2, 3)
        if rounds == ITERS - 1:
            _, keep, gain = momentum(sigma_ratio, spread, contraction)
            gain_ref[...] = jnp.broadcast_to(gain, (1, outs))
            sol_ref[...] += keep * direction[...]
        tree_sides(rounds)
        near_second(field, stage, leaf)
        acc[...] += near_dot(rounds, 3, 4)
        near_finish(field, stage, leaf)
        acc[...] += near_dot(rounds, 4, 5)

        @pl.when(slices)
        def _():
            down_all(rounds, slicers - 1).wait_recv()

        @pl.when(jnp.logical_not(slices))
        def _():
            down_all(rounds, slicers).wait_recv()

        coupled = c_in[rounds].reshape(outs, rank)
        down = lax.dot_general(
            transfer_rows, coupled, (((1,), (1,)), ((), ())), preferred_element_type=f32
        )
        tree_wait(rounds, last_waits)
        level_one = jnp.dot(partners[...], skel[rounds], preferred_element_type=f32)
        far_part = jnp.dot(
            basis_p[...], (level_one + down).astype(bf16), preferred_element_type=f32
        )
        if rounds == ITERS - 1:
            acc[...] += far_part
            break
        residual = res_ref[...] - (acc[...] + far_part)
        res_ref[...] = residual
        rho_next, keep, gain = momentum(sigma_ratio, spread, contraction)
        moved_on = keep * direction[...] + gain * residual
        direction[...] = moved_on
        sol_ref[...] += moved_on
        contraction = rho_next

    near_drain(points, 0, dim)

    @pl.when(slices)
    def _():
        tag_all(2 * slicers - 1).wait_send()
        for rounds in range(ITERS):
            down_all(rounds, n - 1).wait_send()

    @pl.when(jnp.logical_not(slices))
    def _():
        tag_all(2 * slicers).wait_send()

    for rounds in range(ITERS):
        near_drain(wide.at[rounds], rounds + 1, leaf)
        tree_drain(rounds)
        up_all(rounds, slicers).wait_send()


def fused_body(
    coords,
    right_side,
    leaf_perm,
    near_list,
    far_leaves,
    couplings,
    transfer,
    leaf_basis,
    cluster_of,
    far_clusters,
    cluster_couplings,
    ridge_weight,
):
    n = lax.axis_size("dev")
    leaf, dim = coords.shape
    outs = right_side.shape[1]
    rank = transfer.shape[1]
    clusters = cluster_couplings.shape[0]
    slicers = n // 2
    width = outs // slicers
    bf16, f32 = jnp.bfloat16, jnp.float32
    vmem = pl.BlockSpec(memory_space=pltpu.VMEM)
    hbm = pl.BlockSpec(memory_space=pltpu.HBM)
    sem = pltpu.SemaphoreType.DMA
    stages = ITERS + 1

    def stay(array):
        return pltpu.with_memory_space_constraint(array, pltpu.HBM)

    out = jax.ShapeDtypeStruct((leaf, outs), f32)
    base, residual, applied, gain = pl.pallas_call(
        functools.partial(fused_kernel, n),
        out_shape=(out, out, out, jax.ShapeDtypeStruct((1, outs), f32)),
        in_specs=[hbm] * 12,
        out_specs=(vmem, vmem, vmem, vmem),
        scratch_shapes=[
            pltpu.VMEM((5 * dim, leaf), f32),
            pltpu.VMEM((ITERS, 5 * leaf, outs), bf16),
            pltpu.VMEM((leaf, 5 * leaf), bf16),
            pltpu.VMEM((ITERS, n * rank, outs), bf16),
            pltpu.VMEM((ITERS, slicers, width, rank), bf16),
            pltpu.VMEM((ITERS, n, width, rank), bf16),
            pltpu.VMEM((2, n, 1, rank), f32),
            pltpu.VMEM((2 * n, 1, rank), f32),
            pltpu.VMEM((width, clusters * rank), bf16),
            pltpu.VMEM((clusters * rank, clusters * rank), bf16),
            pltpu.VMEM((rank, n * rank), bf16),
            pltpu.VMEM((ITERS, n, width, rank), bf16),
            pltpu.VMEM((ITERS, slicers, width, rank), bf16),
            pltpu.VMEM((leaf, rank), bf16),
            pltpu.VMEM((rank, leaf), bf16),
            pltpu.VMEM((leaf, 6 * dim), bf16),
            pltpu.VMEM((leaf, 128), f32),
            pltpu.VMEM((leaf, outs), f32),
            pltpu.VMEM(leaf_perm.shape, jnp.int32),
            pltpu.VMEM(leaf_basis.shape, bf16),
            pltpu.VMEM(transfer.shape, bf16),
            pltpu.VMEM(couplings.shape, bf16),
            pltpu.VMEM(cluster_couplings.shape, bf16),
            pltpu.VMEM((1, 1), f32),
            pltpu.SMEM((1, 1), jnp.int32),
            pltpu.SMEM(near_list.shape, jnp.int32),
            pltpu.SMEM(far_leaves.shape, jnp.int32),
            pltpu.SMEM(far_clusters.shape, jnp.int32),
            sem((12,)),
            sem((stages, 5, PARTS)),
            sem((stages, 5, PARTS)),
            sem((ITERS, 14)),
            sem((ITERS, n)),
            sem((2 * ITERS + 1,)),
            sem((2 * ITERS + 1,)),
        ],
        compiler_params=pltpu.CompilerParams(
            collective_id=0, has_side_effects=True, vmem_limit_bytes=48 << 20
        ),
        name="fused_solve",
    )(
        stay(coords.T),
        stay(right_side),
        stay(leaf_perm),
        stay(near_list),
        stay(far_leaves),
        stay(couplings),
        stay(transfer),
        stay(leaf_basis),
        cluster_of.reshape(1, 1),
        stay(far_clusters),
        stay(cluster_couplings),
        ridge_weight.reshape(1, 1),
    )
    residual = residual - applied
    return base + gain * residual, residual


def solution(mesh):
    fits = mesh.shape["grp"] == 2 and mesh.shape["dev"] % 4 == 0
    placed = (
        P(("grp", "dev"), None),
        P(("grp", "dev"), None),
        P(("grp", "dev"), None),
        P(("grp", "dev"), None),
        P(("grp", "dev"), None),
        P(("grp", "dev"), None, None, None),
        P(("grp", "dev"), None, None),
        P(("grp", "dev"), None),
        P(("grp", "dev")),
        P("grp", None),
        P("grp", None, None, None),
        P(),
    )
    return jax.shard_map(
        fused_body if fits else body,
        mesh=mesh,
        in_specs=placed,
        out_specs=(P(("grp", "dev"), None), P(("grp", "dev"), None)),
        check_vma=False,
    )
```

```python
import functools

import jax
import jax.numpy as jnp
from jax import lax
from jax.experimental import pallas as pl
from jax.experimental.pallas import tpu as pltpu
from jax.sharding import PartitionSpec as P

MESH = pl.DeviceIdType.MESH
PARTS = 4
EARLY = 2
LATE_TREE = (0,)

REACH = 2
FARREACH = 8
ITERS = 2


kernel_scale = 1.0 / 32.0
spectrum_gap = 0.5
spectrum_top = 8.0


def from_behind(shard, axis, by):
    devices = lax.axis_size(axis)
    pairs = [(i, i + by) for i in range(devices) if 0 <= i + by < devices]
    return lax.ppermute(shard, axis, pairs)


def kernel_block(left_points, right_points):
    inner_products = jnp.dot(
        left_points,
        right_points.T,
        precision=lax.Precision.HIGHEST,
        preferred_element_type=jnp.float32,
    )
    distance = (
        jnp.sum(left_points * left_points, axis=1)[:, None]
        + jnp.sum(right_points * right_points, axis=1)[None, :]
        - 2.0 * inner_products
    )
    return jnp.exp(-kernel_scale * distance).astype(jnp.bfloat16)


def body(
    coords,
    right_side,
    leaf_perm,
    near_list,
    far_leaves,
    couplings,
    transfer,
    leaf_basis,
    cluster_of,
    far_clusters,
    cluster_couplings,
    ridge_weight,
):
    dev_count = lax.axis_size("dev")
    group_index = lax.axis_index("grp")
    leaf_id = group_index * dev_count + lax.axis_index("dev")
    clusters_here = far_clusters.shape[0]
    local_cluster = cluster_of[0] - group_index * clusters_here
    ordering = leaf_perm[0]
    near_offsets = [offset for offset in range(-REACH, REACH + 1) if offset != 0]
    far_offsets = [offset for offset in range(-FARREACH, FARREACH + 1) if abs(offset) > REACH]
    neighbours = [from_behind(coords, "dev", -offset) for offset in near_offsets]
    near_flags = [
        jnp.any((near_list[0] == leaf_id + offset) & (near_list[0] >= 0)).astype(jnp.float32)
        for offset in near_offsets
    ]
    far_hits = jnp.stack(
        [far_leaves[0] == leaf_id + offset for offset in far_offsets], axis=1
    ).astype(jnp.bfloat16)
    own_block = kernel_block(coords, coords)
    near_blocks = [kernel_block(coords, neighbour_points) for neighbour_points in neighbours]
    cluster_slots = (jnp.arange(clusters_here) == local_cluster).astype(jnp.float32)

    def operate(direction):
        values = direction.astype(jnp.bfloat16)
        near_sum = jnp.dot(own_block, values, preferred_element_type=jnp.float32)
        for position in range(len(near_offsets)):
            remote = from_behind(values, "dev", -near_offsets[position])
            block_here = near_blocks[position]
            near_term = near_flags[position] * jnp.dot(
                block_here, remote, preferred_element_type=jnp.float32
            )
            near_sum = near_sum + near_term
        skeleton = lax.dot_general(
            leaf_basis,
            values[ordering],
            (((0,), (0,)), ((), ())),
            preferred_element_type=jnp.float32,
        ).astype(jnp.bfloat16)
        remote_skeletons = jnp.stack(
            [from_behind(skeleton, "dev", -offset) for offset in far_offsets]
        )
        chosen = jnp.einsum(
            "kj,jbo->kbo", far_hits, remote_skeletons, preferred_element_type=jnp.float32
        ).astype(jnp.bfloat16)
        level_one = jnp.einsum(
            "kab,kbo->ao", couplings[0], chosen, preferred_element_type=jnp.float32
        )
        uplift = lax.dot_general(
            transfer[0], skeleton, (((0,), (0,)), ((), ())), preferred_element_type=jnp.float32
        )
        contrib = cluster_slots[:, None, None] * uplift[None]
        column_sums = lax.psum_scatter(contrib, "dev", scatter_dimension=2, tiled=True).astype(
            jnp.bfloat16
        )
        every_column = lax.all_gather(column_sums, "grp", axis=0, tiled=True)
        picked = every_column[far_clusters]
        partial_coupled = jnp.einsum(
            "ckab,ckbo->cao", cluster_couplings, picked, preferred_element_type=jnp.float32
        ).astype(jnp.bfloat16)
        whole_columns = lax.all_gather(partial_coupled, "dev", axis=2, tiled=True)
        coupled = whole_columns[local_cluster]
        downward = jnp.dot(transfer[0], coupled, preferred_element_type=jnp.float32)
        tree_rows = jnp.dot(
            leaf_basis,
            (level_one + downward).astype(jnp.bfloat16),
            preferred_element_type=jnp.float32,
        )
        far_part = jnp.zeros_like(tree_rows).at[ordering].set(tree_rows)
        return ridge_weight * direction + (near_sum + far_part)

    bottom_edge = ridge_weight + spectrum_gap
    top_edge = ridge_weight + spectrum_top
    centre = (top_edge + bottom_edge) / 2.0
    spread = (top_edge - bottom_edge) / 2.0
    sigma_ratio = centre / spread
    contraction = 1.0 / sigma_ratio
    direction = right_side / centre
    solution = direction
    residual = right_side
    for rounds in range(ITERS):
        residual = residual - operate(direction)
        rho_next = 1.0 / (2.0 * sigma_ratio - contraction)
        direction = rho_next * contraction * direction + 2.0 * rho_next / spread * residual
        solution = solution + direction
        contraction = rho_next
    return (solution, residual)


def interval(ridge):
    bottom_edge = ridge + spectrum_gap
    top_edge = ridge + spectrum_top
    centre = (top_edge + bottom_edge) / 2.0
    spread = (top_edge - bottom_edge) / 2.0
    return centre, spread, centre / spread


def momentum(sigma_ratio, spread, contraction):
    rho_next = 1.0 / (2.0 * sigma_ratio - contraction)
    return rho_next, rho_next * contraction, 2.0 * rho_next / spread


def fused_kernel(
    n,
    coords_hbm,
    right_hbm,
    perm_hbm,
    near_hbm,
    far_hbm,
    coup_hbm,
    transfer_hbm,
    basis_hbm,
    cluster_hbm,
    farclus_hbm,
    cluscoup_hbm,
    ridge_hbm,
    sol_ref,
    res_ref,
    acc,
    gain_ref,
    points,
    wide,
    blocks,
    skel,
    up_out,
    up_in,
    tag_in,
    up_tags,
    sums_t,
    pair_map,
    partners,
    c_out,
    c_in,
    basis_p,
    basis_t,
    left_parts,
    left_col,
    direction,
    perm_ref,
    basis_ref,
    transfer_ref,
    coup_ref,
    cluscoup_ref,
    ridge_ref,
    cluster_ref,
    near_ref,
    far_ref,
    farclus_ref,
    load_sem,
    near_send,
    near_recv,
    tree_send,
    tree_recv,
    wide_send,
    wide_recv,
):
    f32, bf16 = jnp.float32, jnp.bfloat16
    group = lax.axis_index("grp")
    me = lax.axis_index("dev")
    other = 1 - group
    chip = lax.div(me, 2)
    core = lax.rem(me, 2)
    row = lax.rem(chip, 2)
    mate = chip * 2 + (1 - core)
    across = me + 2 - 4 * row
    across_mate = mate + 2 - 4 * row
    leaf, outs = right_hbm.shape
    dim = coords_hbm.shape[0]
    rank = transfer_hbm.shape[1]
    clusters = cluscoup_hbm.shape[0]
    planes = n // 4
    plane = lax.div(me, 4)
    slicers = n // 2
    width = outs // slicers
    slices = (row == 1) == (plane < planes // 2)
    my_slice = plane * 2 + core

    def slicer(j):
        side = jnp.where(lax.div(j, 2) < planes // 2, 2, 0)
        return lax.div(j, 2) * 4 + side + lax.rem(j, 2)

    has_z = ((row == 0) & (me >= 4)) | ((row == 1) & (me + 4 < n))
    sends_z = ((row == 0) & (me + 4 < n)) | ((row == 1) & (me >= 4))
    z_target = jnp.where(sends_z, me + 4 - 8 * row, me)

    barrier = pltpu.get_barrier_semaphore()
    for step in range(n):
        place = lax.rem(me + step, n)
        pl.semaphore_signal(
            barrier, inc=1, device_id={"grp": other, "dev": place}, device_id_type=MESH
        )
        if step > 0:
            pl.semaphore_signal(barrier, inc=1, device_id={"dev": place}, device_id_type=MESH)

    loads = {}
    for name, source, target in (
        ("perm", perm_hbm, perm_ref),
        ("cluster", cluster_hbm, cluster_ref),
        ("basis", basis_hbm, basis_ref),
        ("ridge", ridge_hbm, ridge_ref),
        ("right", right_hbm, res_ref),
        ("transfer", transfer_hbm, transfer_ref),
        ("coords", coords_hbm, points.at[pl.ds(0, dim)]),
        ("near", near_hbm, near_ref),
        ("far", far_hbm, far_ref),
        ("farclus", farclus_hbm, farclus_ref),
        ("cluscoup", cluscoup_hbm, cluscoup_ref),
        ("coup", coup_hbm, coup_ref),
    ):
        loads[name] = pltpu.make_async_copy(source, target, load_sem.at[len(loads)])
        loads[name].start()

    def near_copy(buf, stage, source, slot, target, size, part):
        piece = size // PARTS
        return pltpu.make_async_remote_copy(
            src_ref=buf.at[pl.ds(source * size + part * piece, piece)],
            dst_ref=buf.at[pl.ds(slot * size + part * piece, piece)],
            send_sem=near_send.at[stage, slot, part],
            recv_sem=near_recv.at[stage, slot, part],
            device_id={"dev": target},
            device_id_type=MESH,
        )

    def near_start(buf, stage, size):
        for part in range(PARTS):
            near_copy(buf, stage, 0, 2, across, size, part).start()
        for part in range(PARTS):
            near_copy(buf, stage, 0, 1, mate, size, part).start()

        @pl.when(jnp.logical_not(has_z))
        def _():
            buf[pl.ds(3 * size, size), :] = jnp.zeros((size, buf.shape[1]), buf.dtype)

        @pl.when(jnp.logical_not(has_z) & (core == row))
        def _():
            buf[pl.ds(4 * size, size), :] = jnp.zeros((size, buf.shape[1]), buf.dtype)

    def near_relay(buf, stage, size, parts):
        for part in parts:
            near_copy(buf, stage, 0, 2, across, size, part).wait_recv()

            @pl.when(sends_z)
            def _():
                near_copy(buf, stage, 2, 3, z_target, size, part).start()

            @pl.when(core == row)
            def _():
                near_copy(buf, stage, 2, 4, mate, size, part).start()

    def near_second(buf, stage, size):
        for part in range(PARTS):

            @pl.when(has_z)
            def _():
                near_copy(buf, stage, 2, 3, mate, size, part).wait_recv()

            @pl.when(has_z & (core != row))
            def _():
                near_copy(buf, stage, 3, 4, mate, size, part).start()

    def near_first(buf, stage, size):
        for part in range(PARTS):
            near_copy(buf, stage, 0, 1, mate, size, part).wait_recv()

    def near_finish(buf, stage, size):
        for part in range(PARTS):

            @pl.when(has_z | (core != row))
            def _():
                near_copy(buf, stage, 0, 4, mate, size, part).wait_recv()

    def near_drain(buf, stage, size):
        for part in range(PARTS):
            near_copy(buf, stage, 0, 1, mate, size, part).wait_send()
            near_copy(buf, stage, 0, 2, across, size, part).wait_send()

            @pl.when(sends_z)
            def _():
                near_copy(buf, stage, 2, 3, z_target, size, part).wait_send()

            @pl.when(has_z | (core == row))
            def _():
                near_copy(buf, stage, 0, 4, mate, size, part).wait_send()

    heading = 1 - 2 * row

    def inside(owner):
        return (owner >= 0) & (owner < n)

    def tree_copy(rounds, step, owner, target):
        owner = jnp.clip(owner, 0, n - 1)
        place = pl.ds(pl.multiple_of(owner * rank, 16), rank)
        return pltpu.make_async_remote_copy(
            src_ref=skel.at[rounds, place],
            dst_ref=skel.at[rounds, place],
            send_sem=tree_send.at[rounds, step],
            recv_sem=tree_recv.at[rounds, owner],
            device_id={"dev": jnp.clip(target, 0, n - 1)},
            device_id_type=MESH,
        )

    ahead, behind = me + 4 * heading, me - 4 * heading
    own_sends = [
        (inside(ahead), me, ahead),
        (inside(behind), me, behind),
        (inside(ahead + 4 * heading), me, ahead + 4 * heading),
        (inside(behind - 4 * heading), me, behind - 4 * heading),
        (core == row, me, across_mate),
    ]
    lanes = []
    for hops in (1, -1, -2, 2):
        owner = me - 4 * heading * hops
        here = inside(owner)
        if hops == 1:
            sends = [(here, mate), (here, across)]
        elif hops == -1:
            sends = [(here, mate), (here & (core != row), across_mate)]
        elif hops == -2:
            sends = [(here, across), (here & (core == row), mate)]
        else:
            sends = [(here & (core != row), mate)]
        lanes.append((here, owner, [(when, owner, target) for when, target in sends]))
    side_waits = [
        (inside(across + 4 * heading), across + 4 * heading),
        (inside(across - 8 * heading), across - 8 * heading),
    ]
    side_sends = [(here, owner, mate) for here, owner in side_waits]
    last_waits = [
        (core == row, across_mate),
        ((core == 1 - row) & inside(across_mate - 4 * heading), across_mate - 4 * heading),
        (inside(mate - 4), mate - 4),
        (inside(mate + 4), mate + 4),
        ((core == 0) & inside(mate - 8), mate - 8),
        ((core == 1) & inside(mate + 8), mate + 8),
        (inside(across_mate + 4 * heading), across_mate + 4 * heading),
        (inside(across_mate - 8 * heading), across_mate - 8 * heading),
    ]
    every_send = list(own_sends)
    lane_first = []
    for _, _, sends in lanes:
        lane_first.append(len(every_send))
        every_send += sends
    side_first = len(every_send)
    every_send += side_sends

    def tree_go(rounds, first, sends):
        for step, (when, owner, target) in enumerate(sends):

            @pl.when(when)
            def _():
                tree_copy(rounds, first + step, owner, target).start()

    def tree_wait(rounds, waits):
        for when, owner in waits:

            @pl.when(when)
            def _():
                tree_copy(rounds, 0, owner, mate).wait_recv()

    def tree_lanes(rounds, chosen):
        for lane in chosen:
            here, owner, sends = lanes[lane]
            tree_wait(rounds, [(here, owner)])
            tree_go(rounds, lane_first[lane], sends)

    def tree_sides(rounds):
        for side in range(2):
            tree_wait(rounds, side_waits[side : side + 1])
            tree_go(rounds, side_first + side, side_sends[side : side + 1])

    def tree_drain(rounds):
        for step, (when, owner, target) in enumerate(every_send):

            @pl.when(when)
            def _():
                tree_copy(rounds, step, owner, target).wait_send()

    def wide_copy(source, target, sem, device):
        return pltpu.make_async_remote_copy(
            src_ref=source,
            dst_ref=target,
            send_sem=wide_send.at[sem],
            recv_sem=wide_recv.at[sem],
            device_id=device,
            device_id_type=MESH,
        )

    def up_start(rounds):
        for step in range(slicers):
            j = lax.rem(my_slice + slicers // 2 + step, slicers)
            wide_copy(
                up_out.at[rounds, j],
                up_in.at[rounds, me],
                rounds,
                {"grp": other, "dev": slicer(j)},
            ).start()

    def up_all(rounds, count):
        whole = up_in.at[rounds, pl.ds(0, count)]
        return wide_copy(whole, whole, rounds, {"grp": other})

    def tag_start():
        for step in range(slicers):
            place = slicer(lax.rem(my_slice + step, slicers))
            wide_copy(
                tag_in.at[0, me], tag_in.at[1, me], ITERS, {"grp": other, "dev": place}
            ).start()

            @pl.when(place != me)
            def _():
                wide_copy(tag_in.at[0, me], tag_in.at[0, me], ITERS, {"dev": place}).start()

    def tag_all(count):
        whole = up_tags.at[pl.ds(0, count)]
        return wide_copy(whole, whole, ITERS, {"dev": mate})

    def down_start(rounds):
        for step in range(1, n):
            place = lax.rem(me + step, n)
            wide_copy(
                c_out.at[rounds, place],
                c_in.at[rounds, my_slice],
                ITERS + 1 + rounds,
                {"dev": place},
            ).start()

    def down_all(rounds, count):
        whole = c_out.at[rounds, pl.ds(0, count)]
        return wide_copy(whole, whole, ITERS + 1 + rounds, {"dev": mate})

    loads["cluster"].wait()
    local_cluster = cluster_ref[0, 0] - group * clusters
    tag_in[0, me] = jnp.full((1, rank), local_cluster).astype(f32)

    loads["perm"].wait()
    targets = lax.broadcasted_iota(jnp.int32, (leaf, leaf), 0)
    one_hot = jnp.where(targets == perm_ref[...], 1.0, 0.0).astype(bf16)
    loads["basis"].wait()
    placed = jnp.dot(one_hot, basis_ref[...], preferred_element_type=f32)
    basis_p[...] = placed.astype(bf16)
    basis_t[...] = placed.T.astype(bf16)
    loads["ridge"].wait()
    ridge = ridge_ref[...]
    centre, spread, sigma_ratio = interval(ridge)
    contraction = 1.0 / sigma_ratio
    loads["right"].wait()
    start = res_ref[...] / centre
    direction[...] = start
    sol_ref[...] = start
    loads["transfer"].wait()
    transfer_rows = transfer_ref[0]

    def prepare(rounds):
        values = direction[...].astype(bf16)
        wide[rounds, pl.ds(0, leaf), :] = values
        skeleton = jnp.dot(basis_t[...], values, preferred_element_type=f32)
        skel[rounds, pl.ds(pl.multiple_of(me * rank, 16), rank), :] = skeleton.astype(bf16)
        uplift = jnp.dot(
            skeleton.T.astype(bf16), transfer_rows, preferred_element_type=f32
        ).astype(bf16)
        for place in range(slicers):
            up_out[rounds, place] = uplift[place * width : (place + 1) * width, :]

    def send(rounds):
        up_start(rounds)
        near_start(wide.at[rounds], rounds + 1, leaf)
        tree_go(rounds, 0, own_sends)

    def map_clusters():
        for c in range(clusters):
            for place in range(clusters):
                total = jnp.zeros((rank, rank), f32)
                for k in range(farclus_ref.shape[1]):
                    hit = (farclus_ref[c, k] == other * clusters + place).astype(f32)
                    total = total + hit * cluscoup_ref[c, k].astype(f32)
                pair_map[place * rank : (place + 1) * rank, c * rank : (c + 1) * rank] = (
                    total.T.astype(bf16)
                )

    def map_partners():
        for place in range(n):
            total = jnp.zeros((rank, rank), f32)
            for k in range(far_ref.shape[1]):
                hit = (far_ref[0, k] == group * n + place).astype(f32)
                total = total + hit * coup_ref[0, k].astype(f32)
            partners[:, place * rank : (place + 1) * rank] = total.astype(bf16)

            @pl.when((jnp.abs(me - place) <= REACH) | (jnp.abs(me - place) > FARREACH))
            def _():
                for rounds in range(ITERS):
                    if rounds > 0 :
                        skel[rounds, place * rank : (place + 1) * rank, :] = jnp.zeros(
                            (rank, outs), bf16
                        )

                @pl.when(me != place)
                def _():
                    skel[0, place * rank : (place + 1) * rank, :] = jnp.zeros((rank, outs), bf16)

    def couple(rounds):
        @pl.when(slices)
        def _():
            up_all(rounds, n).wait_recv()
            if rounds == 0:
                tag_all(2 * n - 1).wait_recv()
            totals = [jnp.zeros((width, rank), f32) for _ in range(clusters)]
            for place in range(n):
                part = up_in[rounds, place].astype(f32)
                for c in range(clusters):
                    mask = jnp.where(tag_in[1, place] == c, 1.0, 0.0)
                    totals[c] = totals[c] + mask * part
            for c in range(clusters):
                sums_t[:, c * rank : (c + 1) * rank] = totals[c].astype(bf16)
            coupled = jnp.dot(sums_t[...], pair_map[...], preferred_element_type=f32)
            for place in range(n):
                pick = jnp.zeros((width, rank), f32)
                for c in range(clusters):
                    mask = jnp.where(tag_in[0, place] == c, 1.0, 0.0)
                    pick = pick + mask * coupled[:, c * rank : (c + 1) * rank]
                c_out[rounds, place] = pick.astype(bf16)
            c_in[rounds, my_slice] = c_out[rounds, me]
            down_start(rounds)

    loads["coords"].wait()
    log2e = 1.4426950408889634

    def split(x):
        high = x.astype(bf16).astype(f32)
        middle = (x - high).astype(bf16).astype(f32)
        return high, middle, x - high - middle

    own = points[pl.ds(0, dim), :]
    high, middle, low = split(own * (2.0 * kernel_scale * log2e))
    left_parts[...] = (
        jnp.concatenate([high, high, middle, middle, high, low], axis=0).T.astype(bf16)
    )
    left_sq = jnp.sum(own * own, axis=0, keepdims=True) * (kernel_scale * log2e)
    left_col[...] = jnp.broadcast_to(left_sq, (128, leaf)).T

    def fill_block(slot, source):
        right = points[pl.ds(slot * dim, dim), :]
        lift = jnp.sum(right * right, axis=0, keepdims=True) * (kernel_scale * log2e)
        if source is not None:
            wanted = group * n + source
            hit = jnp.float32(0.0)
            for k in range(near_ref.shape[1]):
                listed = (near_ref[0, k] == wanted) & (near_ref[0, k] >= 0)
                hit = hit + listed.astype(f32)
            lift = lift + (1.0 - hit) * 1e4
        high, middle, low = split(right)
        right_parts = jnp.concatenate([high, middle, high, middle, low, high], axis=0)
        inner = jnp.dot(left_parts[...], right_parts.astype(bf16), preferred_element_type=f32)
        block = jnp.exp2(inner - (left_col[:, 0:1] + lift))
        blocks[:, slot * leaf : (slot + 1) * leaf] = block.astype(bf16)

    def near_dot(rounds, first, last):
        return jnp.dot(
            blocks[:, first * leaf : last * leaf],
            wide[rounds, first * leaf : last * leaf, :],
            preferred_element_type=f32,
        )

    prepare(0)
    pl.semaphore_wait(barrier, 2 * n - 1)
    up_start(0)
    tag_start()
    near_start(points, 0, dim)
    near_start(wide.at[0], 1, leaf)
    tree_go(0, 0, own_sends)
    parts = range(PARTS)
    for rounds in range(ITERS):
        stage = rounds + 1
        field = wide.at[rounds]
        if rounds > 0:
            prepare(rounds)
            send(rounds)
            near_first(field, stage, leaf)
            acc[...] = ridge * direction[...] + near_dot(rounds, 0, 2)
            near_relay(field, stage, leaf, parts[:EARLY])
            tree_lanes(rounds, (0, 1))
            couple(rounds)
            near_relay(field, stage, leaf, parts[EARLY:])
            tree_lanes(rounds, (2, 3))
        else:
            fill_block(0, None)
            loads["near"].wait()
            near_first(points, 0, dim)
            fill_block(1, mate)
            loads["farclus"].wait()
            loads["cluscoup"].wait()
            map_clusters()
            loads["far"].wait()
            loads["coup"].wait()
            map_partners()
            near_relay(points, 0, dim, parts[:1])
            near_first(field, stage, leaf)
            acc[...] = ridge * direction[...] + near_dot(rounds, 0, 2)
            near_relay(points, 0, dim, parts[1:])
            tree_lanes(rounds, (0, 1))
            couple(rounds)
            fill_block(2, across)
            near_relay(field, stage, leaf, parts[:EARLY])
            tree_lanes(rounds, (2,))
            near_second(points, 0, dim)
            near_relay(field, stage, leaf, parts[EARLY:])
            fill_block(3, me - 2 + 4 * row)
            near_finish(points, 0, dim)
            fill_block(4, me - 1 + 2 * core)
            tree_lanes(rounds, (3,))
        acc[...] += near_dot(rounds, 2, 3)
        if rounds == ITERS - 1:
            _, keep, gain = momentum(sigma_ratio, spread, contraction)
            gain_ref[...] = jnp.broadcast_to(gain, (1, outs))
            sol_ref[...] += keep * direction[...]
        tree_sides(rounds)
        near_second(field, stage, leaf)
        acc[...] += near_dot(rounds, 3, 4)
        if rounds in LATE_TREE:
            near_finish(field, stage, leaf)
            acc[...] += near_dot(rounds, 4, 5)

        @pl.when(slices)
        def _():
            down_all(rounds, slicers - 1).wait_recv()

        @pl.when(jnp.logical_not(slices))
        def _():
            down_all(rounds, slicers).wait_recv()

        coupled = c_in[rounds].reshape(outs, rank)
        down = lax.dot_general(
            transfer_rows, coupled, (((1,), (1,)), ((), ())), preferred_element_type=f32
        )
        tree_wait(rounds, last_waits)
        level_one = jnp.dot(partners[...], skel[rounds], preferred_element_type=f32)
        far_part = jnp.dot(
            basis_p[...], (level_one + down).astype(bf16), preferred_element_type=f32
        )
        acc[...] += far_part
        if rounds not in LATE_TREE:
            near_finish(field, stage, leaf)
            acc[...] += near_dot(rounds, 4, 5)
        if rounds == ITERS - 1:
            break
        residual = res_ref[...] - acc[...]
        res_ref[...] = residual
        rho_next, keep, gain = momentum(sigma_ratio, spread, contraction)
        moved_on = keep * direction[...] + gain * residual
        direction[...] = moved_on
        sol_ref[...] += moved_on
        contraction = rho_next

    near_drain(points, 0, dim)

    @pl.when(slices)
    def _():
        tag_all(2 * slicers - 1).wait_send()
        for rounds in range(ITERS):
            down_all(rounds, n - 1).wait_send()

    @pl.when(jnp.logical_not(slices))
    def _():
        tag_all(2 * slicers).wait_send()

    for rounds in range(ITERS):
        near_drain(wide.at[rounds], rounds + 1, leaf)
        tree_drain(rounds)
        up_all(rounds, slicers).wait_send()


def fused_body(
    coords,
    right_side,
    leaf_perm,
    near_list,
    far_leaves,
    couplings,
    transfer,
    leaf_basis,
    cluster_of,
    far_clusters,
    cluster_couplings,
    ridge_weight,
):
    n = lax.axis_size("dev")
    leaf, dim = coords.shape
    outs = right_side.shape[1]
    rank = transfer.shape[1]
    clusters = cluster_couplings.shape[0]
    slicers = n // 2
    width = outs // slicers
    bf16, f32 = jnp.bfloat16, jnp.float32
    vmem = pl.BlockSpec(memory_space=pltpu.VMEM)
    hbm = pl.BlockSpec(memory_space=pltpu.HBM)
    sem = pltpu.SemaphoreType.DMA
    stages = ITERS + 1

    def stay(array):
        return pltpu.with_memory_space_constraint(array, pltpu.HBM)

    out = jax.ShapeDtypeStruct((leaf, outs), f32)
    base, residual, applied, gain = pl.pallas_call(
        functools.partial(fused_kernel, n),
        out_shape=(out, out, out, jax.ShapeDtypeStruct((1, outs), f32)),
        in_specs=[hbm] * 12,
        out_specs=(vmem, vmem, vmem, vmem),
        scratch_shapes=[
            pltpu.VMEM((5 * dim, leaf), f32),
            pltpu.VMEM((ITERS, 5 * leaf, outs), bf16),
            pltpu.VMEM((leaf, 5 * leaf), bf16),
            pltpu.VMEM((ITERS, n * rank, outs), bf16),
            pltpu.VMEM((ITERS, slicers, width, rank), bf16),
            pltpu.VMEM((ITERS, n, width, rank), bf16),
            pltpu.VMEM((2, n, 1, rank), f32),
            pltpu.VMEM((2 * n, 1, rank), f32),
            pltpu.VMEM((width, clusters * rank), bf16),
            pltpu.VMEM((clusters * rank, clusters * rank), bf16),
            pltpu.VMEM((rank, n * rank), bf16),
            pltpu.VMEM((ITERS, n, width, rank), bf16),
            pltpu.VMEM((ITERS, slicers, width, rank), bf16),
            pltpu.VMEM((leaf, rank), bf16),
            pltpu.VMEM((rank, leaf), bf16),
            pltpu.VMEM((leaf, 6 * dim), bf16),
            pltpu.VMEM((leaf, 128), f32),
            pltpu.VMEM((leaf, outs), f32),
            pltpu.VMEM(leaf_perm.shape, jnp.int32),
            pltpu.VMEM(leaf_basis.shape, bf16),
            pltpu.VMEM(transfer.shape, bf16),
            pltpu.VMEM(couplings.shape, bf16),
            pltpu.VMEM(cluster_couplings.shape, bf16),
            pltpu.VMEM((1, 1), f32),
            pltpu.SMEM((1, 1), jnp.int32),
            pltpu.SMEM(near_list.shape, jnp.int32),
            pltpu.SMEM(far_leaves.shape, jnp.int32),
            pltpu.SMEM(far_clusters.shape, jnp.int32),
            sem((12,)),
            sem((stages, 5, PARTS)),
            sem((stages, 5, PARTS)),
            sem((ITERS, 14)),
            sem((ITERS, n)),
            sem((2 * ITERS + 1,)),
            sem((2 * ITERS + 1,)),
        ],
        compiler_params=pltpu.CompilerParams(
            collective_id=0, has_side_effects=True, vmem_limit_bytes=48 << 20
        ),
        name="fused_solve",
    )(
        stay(coords.T),
        stay(right_side),
        stay(leaf_perm),
        stay(near_list),
        stay(far_leaves),
        stay(couplings),
        stay(transfer),
        stay(leaf_basis),
        cluster_of.reshape(1, 1),
        stay(far_clusters),
        stay(cluster_couplings),
        ridge_weight.reshape(1, 1),
    )
    residual = residual - applied
    return base + gain * residual, residual


def solution(mesh):
    fits = mesh.shape["grp"] == 2 and mesh.shape["dev"] % 4 == 0
    placed = (
        P(("grp", "dev"), None),
        P(("grp", "dev"), None),
        P(("grp", "dev"), None),
        P(("grp", "dev"), None),
        P(("grp", "dev"), None),
        P(("grp", "dev"), None, None, None),
        P(("grp", "dev"), None, None),
        P(("grp", "dev"), None),
        P(("grp", "dev")),
        P("grp", None),
        P("grp", None, None, None),
        P(),
    )
    return jax.shard_map(
        fused_body if fits else body,
        mesh=mesh,
        in_specs=placed,
        out_specs=(P(("grp", "dev"), None), P(("grp", "dev"), None)),
        check_vma=False,
    )
```

```python
import functools

import jax
import jax.numpy as jnp
from jax import lax
from jax.experimental import pallas as pl
from jax.experimental.pallas import tpu as pltpu
from jax.sharding import PartitionSpec as P

MESH = pl.DeviceIdType.MESH
PARTS = 4
EARLY = 2
LATE_TREE = (0,)

REACH = 2
FARREACH = 8
ITERS = 2


kernel_scale = 1.0 / 32.0
spectrum_gap = 0.5
spectrum_top = 8.0


def from_behind(shard, axis, by):
    devices = lax.axis_size(axis)
    pairs = [(i, i + by) for i in range(devices) if 0 <= i + by < devices]
    return lax.ppermute(shard, axis, pairs)


def kernel_block(left_points, right_points):
    inner_products = jnp.dot(
        left_points,
        right_points.T,
        precision=lax.Precision.HIGHEST,
        preferred_element_type=jnp.float32,
    )
    distance = (
        jnp.sum(left_points * left_points, axis=1)[:, None]
        + jnp.sum(right_points * right_points, axis=1)[None, :]
        - 2.0 * inner_products
    )
    return jnp.exp(-kernel_scale * distance).astype(jnp.bfloat16)


def body(
    coords,
    right_side,
    leaf_perm,
    near_list,
    far_leaves,
    couplings,
    transfer,
    leaf_basis,
    cluster_of,
    far_clusters,
    cluster_couplings,
    ridge_weight,
):
    dev_count = lax.axis_size("dev")
    group_index = lax.axis_index("grp")
    leaf_id = group_index * dev_count + lax.axis_index("dev")
    clusters_here = far_clusters.shape[0]
    local_cluster = cluster_of[0] - group_index * clusters_here
    ordering = leaf_perm[0]
    near_offsets = [offset for offset in range(-REACH, REACH + 1) if offset != 0]
    far_offsets = [offset for offset in range(-FARREACH, FARREACH + 1) if abs(offset) > REACH]
    neighbours = [from_behind(coords, "dev", -offset) for offset in near_offsets]
    near_flags = [
        jnp.any((near_list[0] == leaf_id + offset) & (near_list[0] >= 0)).astype(jnp.float32)
        for offset in near_offsets
    ]
    far_hits = jnp.stack(
        [far_leaves[0] == leaf_id + offset for offset in far_offsets], axis=1
    ).astype(jnp.bfloat16)
    own_block = kernel_block(coords, coords)
    near_blocks = [kernel_block(coords, neighbour_points) for neighbour_points in neighbours]
    cluster_slots = (jnp.arange(clusters_here) == local_cluster).astype(jnp.float32)

    def operate(direction):
        values = direction.astype(jnp.bfloat16)
        near_sum = jnp.dot(own_block, values, preferred_element_type=jnp.float32)
        for position in range(len(near_offsets)):
            remote = from_behind(values, "dev", -near_offsets[position])
            block_here = near_blocks[position]
            near_term = near_flags[position] * jnp.dot(
                block_here, remote, preferred_element_type=jnp.float32
            )
            near_sum = near_sum + near_term
        skeleton = lax.dot_general(
            leaf_basis,
            values[ordering],
            (((0,), (0,)), ((), ())),
            preferred_element_type=jnp.float32,
        ).astype(jnp.bfloat16)
        remote_skeletons = jnp.stack(
            [from_behind(skeleton, "dev", -offset) for offset in far_offsets]
        )
        chosen = jnp.einsum(
            "kj,jbo->kbo", far_hits, remote_skeletons, preferred_element_type=jnp.float32
        ).astype(jnp.bfloat16)
        level_one = jnp.einsum(
            "kab,kbo->ao", couplings[0], chosen, preferred_element_type=jnp.float32
        )
        uplift = lax.dot_general(
            transfer[0], skeleton, (((0,), (0,)), ((), ())), preferred_element_type=jnp.float32
        )
        contrib = cluster_slots[:, None, None] * uplift[None]
        column_sums = lax.psum_scatter(contrib, "dev", scatter_dimension=2, tiled=True).astype(
            jnp.bfloat16
        )
        every_column = lax.all_gather(column_sums, "grp", axis=0, tiled=True)
        picked = every_column[far_clusters]
        partial_coupled = jnp.einsum(
            "ckab,ckbo->cao", cluster_couplings, picked, preferred_element_type=jnp.float32
        ).astype(jnp.bfloat16)
        whole_columns = lax.all_gather(partial_coupled, "dev", axis=2, tiled=True)
        coupled = whole_columns[local_cluster]
        downward = jnp.dot(transfer[0], coupled, preferred_element_type=jnp.float32)
        tree_rows = jnp.dot(
            leaf_basis,
            (level_one + downward).astype(jnp.bfloat16),
            preferred_element_type=jnp.float32,
        )
        far_part = jnp.zeros_like(tree_rows).at[ordering].set(tree_rows)
        return ridge_weight * direction + (near_sum + far_part)

    bottom_edge = ridge_weight + spectrum_gap
    top_edge = ridge_weight + spectrum_top
    centre = (top_edge + bottom_edge) / 2.0
    spread = (top_edge - bottom_edge) / 2.0
    sigma_ratio = centre / spread
    contraction = 1.0 / sigma_ratio
    direction = right_side / centre
    solution = direction
    residual = right_side
    for rounds in range(ITERS):
        residual = residual - operate(direction)
        rho_next = 1.0 / (2.0 * sigma_ratio - contraction)
        direction = rho_next * contraction * direction + 2.0 * rho_next / spread * residual
        solution = solution + direction
        contraction = rho_next
    return (solution, residual)


def interval(ridge):
    bottom_edge = ridge + spectrum_gap
    top_edge = ridge + spectrum_top
    centre = (top_edge + bottom_edge) / 2.0
    spread = (top_edge - bottom_edge) / 2.0
    return centre, spread, centre / spread


def momentum(sigma_ratio, spread, contraction):
    rho_next = 1.0 / (2.0 * sigma_ratio - contraction)
    return rho_next, rho_next * contraction, 2.0 * rho_next / spread


def fused_kernel(
    n,
    coords_hbm,
    right_hbm,
    perm_hbm,
    near_hbm,
    far_hbm,
    coup_hbm,
    transfer_hbm,
    basis_hbm,
    cluster_hbm,
    farclus_hbm,
    cluscoup_hbm,
    ridge_hbm,
    sol_ref,
    res_ref,
    acc,
    gain_ref,
    points,
    wide,
    blocks,
    skel,
    up_out,
    up_in,
    tag_in,
    up_tags,
    sums_t,
    pair_map,
    partners,
    c_out,
    c_in,
    basis_p,
    basis_t,
    left_parts,
    left_col,
    direction,
    perm_ref,
    basis_ref,
    transfer_ref,
    coup_ref,
    cluscoup_ref,
    ridge_ref,
    cluster_ref,
    near_ref,
    far_ref,
    farclus_ref,
    load_sem,
    near_send,
    near_recv,
    tree_send,
    tree_recv,
    wide_send,
    wide_recv,
):
    f32, bf16 = jnp.float32, jnp.bfloat16
    group = lax.axis_index("grp")
    me = lax.axis_index("dev")
    other = 1 - group
    chip = lax.div(me, 2)
    core = lax.rem(me, 2)
    row = lax.rem(chip, 2)
    mate = chip * 2 + (1 - core)
    across = me + 2 - 4 * row
    across_mate = mate + 2 - 4 * row
    leaf, outs = right_hbm.shape
    dim = coords_hbm.shape[0]
    rank = transfer_hbm.shape[1]
    clusters = cluscoup_hbm.shape[0]
    planes = n // 4
    plane = lax.div(me, 4)
    slicers = n // 2
    width = outs // slicers
    slices = (row == 1) == (plane < planes // 2)
    my_slice = plane * 2 + core

    def slicer(j):
        side = jnp.where(lax.div(j, 2) < planes // 2, 2, 0)
        return lax.div(j, 2) * 4 + side + lax.rem(j, 2)

    has_z = ((row == 0) & (me >= 4)) | ((row == 1) & (me + 4 < n))
    sends_z = ((row == 0) & (me + 4 < n)) | ((row == 1) & (me >= 4))
    z_target = jnp.where(sends_z, me + 4 - 8 * row, me)

    barrier = pltpu.get_barrier_semaphore()
    for step in range(n):
        place = lax.rem(me + step, n)
        pl.semaphore_signal(
            barrier, inc=1, device_id={"grp": other, "dev": place}, device_id_type=MESH
        )
        if step > 0:
            pl.semaphore_signal(barrier, inc=1, device_id={"dev": place}, device_id_type=MESH)

    loads = {}
    for name, source, target in (
        ("perm", perm_hbm, perm_ref),
        ("cluster", cluster_hbm, cluster_ref),
        ("basis", basis_hbm, basis_ref),
        ("ridge", ridge_hbm, ridge_ref),
        ("right", right_hbm, res_ref),
        ("transfer", transfer_hbm, transfer_ref),
        ("coords", coords_hbm, points.at[pl.ds(0, dim)]),
        ("near", near_hbm, near_ref),
        ("far", far_hbm, far_ref),
        ("farclus", farclus_hbm, farclus_ref),
        ("cluscoup", cluscoup_hbm, cluscoup_ref),
        ("coup", coup_hbm, coup_ref),
    ):
        loads[name] = pltpu.make_async_copy(source, target, load_sem.at[len(loads)])
        loads[name].start()

    def near_copy(buf, stage, source, slot, target, size, part):
        piece = size // PARTS
        return pltpu.make_async_remote_copy(
            src_ref=buf.at[pl.ds(source * size + part * piece, piece)],
            dst_ref=buf.at[pl.ds(slot * size + part * piece, piece)],
            send_sem=near_send.at[stage, slot, part],
            recv_sem=near_recv.at[stage, slot, part],
            device_id={"dev": target},
            device_id_type=MESH,
        )

    def near_start(buf, stage, size):
        for part in range(PARTS):
            near_copy(buf, stage, 0, 2, across, size, part).start()
        for part in range(PARTS):
            near_copy(buf, stage, 0, 1, mate, size, part).start()

        @pl.when(jnp.logical_not(has_z))
        def _():
            buf[pl.ds(3 * size, size), :] = jnp.zeros((size, buf.shape[1]), buf.dtype)

        @pl.when(jnp.logical_not(has_z) & (core == row))
        def _():
            buf[pl.ds(4 * size, size), :] = jnp.zeros((size, buf.shape[1]), buf.dtype)

    def near_relay(buf, stage, size, parts):
        for part in parts:
            near_copy(buf, stage, 0, 2, across, size, part).wait_recv()

            @pl.when(sends_z)
            def _():
                near_copy(buf, stage, 2, 3, z_target, size, part).start()

            @pl.when(core == row)
            def _():
                near_copy(buf, stage, 2, 4, mate, size, part).start()

    def near_second(buf, stage, size):
        for part in range(PARTS):

            @pl.when(has_z)
            def _():
                near_copy(buf, stage, 2, 3, mate, size, part).wait_recv()

            @pl.when(has_z & (core != row))
            def _():
                near_copy(buf, stage, 3, 4, mate, size, part).start()

    def near_first(buf, stage, size):
        for part in range(PARTS):
            near_copy(buf, stage, 0, 1, mate, size, part).wait_recv()

    def near_finish(buf, stage, size):
        for part in range(PARTS):

            @pl.when(has_z | (core != row))
            def _():
                near_copy(buf, stage, 0, 4, mate, size, part).wait_recv()

    def near_drain(buf, stage, size):
        for part in range(PARTS):
            near_copy(buf, stage, 0, 1, mate, size, part).wait_send()
            near_copy(buf, stage, 0, 2, across, size, part).wait_send()

            @pl.when(sends_z)
            def _():
                near_copy(buf, stage, 2, 3, z_target, size, part).wait_send()

            @pl.when(has_z | (core == row))
            def _():
                near_copy(buf, stage, 0, 4, mate, size, part).wait_send()

    heading = 1 - 2 * row

    def inside(owner):
        return (owner >= 0) & (owner < n)

    def tree_copy(rounds, step, owner, target):
        owner = jnp.clip(owner, 0, n - 1)
        place = pl.ds(pl.multiple_of(owner * rank, 16), rank)
        return pltpu.make_async_remote_copy(
            src_ref=skel.at[rounds, place],
            dst_ref=skel.at[rounds, place],
            send_sem=tree_send.at[rounds, step],
            recv_sem=tree_recv.at[rounds, owner],
            device_id={"dev": jnp.clip(target, 0, n - 1)},
            device_id_type=MESH,
        )

    ahead, behind = me + 4 * heading, me - 4 * heading
    own_sends = [
        (inside(ahead), me, ahead),
        (inside(behind), me, behind),
        (inside(ahead + 4 * heading), me, ahead + 4 * heading),
        (inside(behind - 4 * heading), me, behind - 4 * heading),
        (core == row, me, across_mate),
    ]
    lanes = []
    for hops in (1, -1, -2, 2):
        owner = me - 4 * heading * hops
        here = inside(owner)
        if hops == 1:
            sends = [(here, mate), (here, across)]
        elif hops == -1:
            sends = [(here, mate), (here & (core != row), across_mate)]
        elif hops == -2:
            sends = [(here, across), (here & (core == row), mate)]
        else:
            sends = [(here & (core != row), mate)]
        lanes.append((here, owner, [(when, owner, target) for when, target in sends]))
    side_waits = [
        (inside(across + 4 * heading), across + 4 * heading),
        (inside(across - 8 * heading), across - 8 * heading),
    ]
    side_sends = [(here, owner, mate) for here, owner in side_waits]
    last_waits = [
        (core == row, across_mate),
        ((core == 1 - row) & inside(across_mate - 4 * heading), across_mate - 4 * heading),
        (inside(mate - 4), mate - 4),
        (inside(mate + 4), mate + 4),
        ((core == 0) & inside(mate - 8), mate - 8),
        ((core == 1) & inside(mate + 8), mate + 8),
        (inside(across_mate + 4 * heading), across_mate + 4 * heading),
        (inside(across_mate - 8 * heading), across_mate - 8 * heading),
    ]
    every_send = list(own_sends)
    lane_first = []
    for _, _, sends in lanes:
        lane_first.append(len(every_send))
        every_send += sends
    side_first = len(every_send)
    every_send += side_sends

    def tree_go(rounds, first, sends):
        for step, (when, owner, target) in enumerate(sends):

            @pl.when(when)
            def _():
                tree_copy(rounds, first + step, owner, target).start()

    def tree_wait(rounds, waits):
        for when, owner in waits:

            @pl.when(when)
            def _():
                tree_copy(rounds, 0, owner, mate).wait_recv()

    def tree_lanes(rounds, chosen):
        for lane in chosen:
            here, owner, sends = lanes[lane]
            tree_wait(rounds, [(here, owner)])
            tree_go(rounds, lane_first[lane], sends)

    def tree_sides(rounds):
        for side in range(2):
            tree_wait(rounds, side_waits[side : side + 1])
            tree_go(rounds, side_first + side, side_sends[side : side + 1])

    def tree_drain(rounds):
        for step, (when, owner, target) in enumerate(every_send):

            @pl.when(when)
            def _():
                tree_copy(rounds, step, owner, target).wait_send()

    def wide_copy(source, target, sem, device):
        return pltpu.make_async_remote_copy(
            src_ref=source,
            dst_ref=target,
            send_sem=wide_send.at[sem],
            recv_sem=wide_recv.at[sem],
            device_id=device,
            device_id_type=MESH,
        )

    def up_start(rounds):
        for step in range(slicers):
            j = lax.rem(my_slice + slicers // 2 + step, slicers)
            wide_copy(
                up_out.at[rounds, j],
                up_in.at[rounds, me],
                rounds,
                {"grp": other, "dev": slicer(j)},
            ).start()

    def up_all(rounds, count):
        whole = up_in.at[rounds, pl.ds(0, count)]
        return wide_copy(whole, whole, rounds, {"grp": other})

    def tag_start():
        for step in range(slicers):
            place = slicer(lax.rem(my_slice + step, slicers))
            wide_copy(
                tag_in.at[0, me], tag_in.at[1, me], ITERS, {"grp": other, "dev": place}
            ).start()

            @pl.when(place != me)
            def _():
                wide_copy(tag_in.at[0, me], tag_in.at[0, me], ITERS, {"dev": place}).start()

    def tag_all(count):
        whole = up_tags.at[pl.ds(0, count)]
        return wide_copy(whole, whole, ITERS, {"dev": mate})

    def down_start(rounds):
        for step in range(1, n):
            place = lax.rem(me + step, n)
            wide_copy(
                c_out.at[rounds, place],
                c_in.at[rounds, my_slice],
                ITERS + 1 + rounds,
                {"dev": place},
            ).start()

    def down_all(rounds, count):
        whole = c_out.at[rounds, pl.ds(0, count)]
        return wide_copy(whole, whole, ITERS + 1 + rounds, {"dev": mate})

    loads["cluster"].wait()
    local_cluster = cluster_ref[0, 0] - group * clusters
    tag_in[0, me] = jnp.full((1, rank), local_cluster).astype(f32)

    loads["perm"].wait()
    targets = lax.broadcasted_iota(jnp.int32, (leaf, leaf), 0)
    one_hot = jnp.where(targets == perm_ref[...], 1.0, 0.0).astype(bf16)
    loads["basis"].wait()
    placed = jnp.dot(one_hot, basis_ref[...], preferred_element_type=f32)
    basis_p[...] = placed.astype(bf16)
    basis_t[...] = placed.T.astype(bf16)
    loads["ridge"].wait()
    ridge = ridge_ref[...]
    centre, spread, sigma_ratio = interval(ridge)
    contraction = 1.0 / sigma_ratio
    loads["right"].wait()
    start = res_ref[...] / centre
    direction[...] = start
    sol_ref[...] = start
    loads["transfer"].wait()
    transfer_rows = transfer_ref[0]

    def prepare(rounds):
        values = direction[...].astype(bf16)
        wide[rounds, pl.ds(0, leaf), :] = values
        skeleton = jnp.dot(basis_t[...], values, preferred_element_type=f32)
        skel[rounds, pl.ds(pl.multiple_of(me * rank, 16), rank), :] = skeleton.astype(bf16)
        uplift = jnp.dot(
            skeleton.T.astype(bf16), transfer_rows, preferred_element_type=f32
        ).astype(bf16)
        for place in range(slicers):
            up_out[rounds, place] = uplift[place * width : (place + 1) * width, :]

    def send(rounds):
        up_start(rounds)
        near_start(wide.at[rounds], rounds + 1, leaf)
        tree_go(rounds, 0, own_sends)

    def map_clusters():
        for c in range(clusters):
            for place in range(clusters):
                total = jnp.zeros((rank, rank), f32)
                for k in range(farclus_ref.shape[1]):
                    hit = (farclus_ref[c, k] == other * clusters + place).astype(f32)
                    total = total + hit * cluscoup_ref[c, k].astype(f32)
                pair_map[place * rank : (place + 1) * rank, c * rank : (c + 1) * rank] = (
                    total.T.astype(bf16)
                )

    def map_partners():
        for place in range(n):
            total = jnp.zeros((rank, rank), f32)
            for k in range(far_ref.shape[1]):
                hit = (far_ref[0, k] == group * n + place).astype(f32)
                total = total + hit * coup_ref[0, k].astype(f32)
            partners[:, place * rank : (place + 1) * rank] = total.astype(bf16)

            @pl.when((jnp.abs(me - place) <= REACH) | (jnp.abs(me - place) > FARREACH))
            def _():
                for rounds in range(ITERS):
                    if rounds > 0 :
                        skel[rounds, place * rank : (place + 1) * rank, :] = jnp.zeros(
                            (rank, outs), bf16
                        )

                @pl.when(me != place)
                def _():
                    skel[0, place * rank : (place + 1) * rank, :] = jnp.zeros((rank, outs), bf16)

    def couple(rounds):
        @pl.when(slices)
        def _():
            up_all(rounds, n).wait_recv()
            if rounds == 0:
                tag_all(2 * n - 1).wait_recv()
            totals = [jnp.zeros((width, rank), f32) for _ in range(clusters)]
            for place in range(n):
                part = up_in[rounds, place].astype(f32)
                for c in range(clusters):
                    mask = jnp.where(tag_in[1, place] == c, 1.0, 0.0)
                    totals[c] = totals[c] + mask * part
            for c in range(clusters):
                sums_t[:, c * rank : (c + 1) * rank] = totals[c].astype(bf16)
            coupled = jnp.dot(sums_t[...], pair_map[...], preferred_element_type=f32)
            for place in range(n):
                pick = jnp.zeros((width, rank), f32)
                for c in range(clusters):
                    mask = jnp.where(tag_in[0, place] == c, 1.0, 0.0)
                    pick = pick + mask * coupled[:, c * rank : (c + 1) * rank]
                c_out[rounds, place] = pick.astype(bf16)
            c_in[rounds, my_slice] = c_out[rounds, me]
            down_start(rounds)

    loads["coords"].wait()
    log2e = 1.4426950408889634

    def split(x):
        high = x.astype(bf16).astype(f32)
        middle = (x - high).astype(bf16).astype(f32)
        return high, middle, x - high - middle

    own = points[pl.ds(0, dim), :]
    high, middle, low = split(own * (2.0 * kernel_scale * log2e))
    left_parts[...] = (
        jnp.concatenate([high, high, middle, middle, high, low], axis=0).T.astype(bf16)
    )
    left_sq = jnp.sum(own * own, axis=0, keepdims=True) * (kernel_scale * log2e)
    left_col[...] = jnp.broadcast_to(left_sq, (128, leaf)).T

    def fill_block(slot, source):
        right = points[pl.ds(slot * dim, dim), :]
        lift = jnp.sum(right * right, axis=0, keepdims=True) * (kernel_scale * log2e)
        if source is not None:
            wanted = group * n + source
            hit = jnp.float32(0.0)
            for k in range(near_ref.shape[1]):
                listed = (near_ref[0, k] == wanted) & (near_ref[0, k] >= 0)
                hit = hit + listed.astype(f32)
            lift = lift + (1.0 - hit) * 1e4
        high, middle, low = split(right)
        right_parts = jnp.concatenate([high, middle, high, middle, low, high], axis=0)
        inner = jnp.dot(left_parts[...], right_parts.astype(bf16), preferred_element_type=f32)
        block = jnp.exp2(inner - (left_col[:, 0:1] + lift))
        blocks[:, slot * leaf : (slot + 1) * leaf] = block.astype(bf16)

    def near_dot(rounds, first, last):
        return jnp.dot(
            blocks[:, first * leaf : last * leaf],
            wide[rounds, first * leaf : last * leaf, :],
            preferred_element_type=f32,
        )

    prepare(0)
    pl.semaphore_wait(barrier, 2 * n - 1)
    up_start(0)
    tag_start()
    near_start(points, 0, dim)
    near_start(wide.at[0], 1, leaf)
    tree_go(0, 0, own_sends)
    parts = range(PARTS)
    for rounds in range(ITERS):
        stage = rounds + 1
        field = wide.at[rounds]
        if rounds > 0:
            prepare(rounds)
            send(rounds)
            near_first(field, stage, leaf)
            acc[...] = ridge * direction[...] + near_dot(rounds, 0, 2)
            tree_lanes(rounds, (0,))
            near_relay(field, stage, leaf, parts[:EARLY])
            couple(rounds)
            tree_lanes(rounds, (2,))
            near_relay(field, stage, leaf, parts[EARLY:])
            tree_lanes(rounds, (1, 3))
        else:
            fill_block(0, None)
            loads["near"].wait()
            near_first(points, 0, dim)
            fill_block(1, mate)
            loads["farclus"].wait()
            loads["cluscoup"].wait()
            map_clusters()
            loads["far"].wait()
            loads["coup"].wait()
            map_partners()
            near_relay(points, 0, dim, parts[:1])
            near_first(field, stage, leaf)
            acc[...] = ridge * direction[...] + near_dot(rounds, 0, 2)
            near_relay(points, 0, dim, parts[1:])
            tree_lanes(rounds, (0, 1))
            couple(rounds)
            fill_block(2, across)
            near_relay(field, stage, leaf, parts[:EARLY])
            tree_lanes(rounds, (2,))
            near_second(points, 0, dim)
            near_relay(field, stage, leaf, parts[EARLY:])
            fill_block(3, me - 2 + 4 * row)
            near_finish(points, 0, dim)
            fill_block(4, me - 1 + 2 * core)
            tree_lanes(rounds, (3,))
        acc[...] += near_dot(rounds, 2, 3)
        if rounds == ITERS - 1:
            _, keep, gain = momentum(sigma_ratio, spread, contraction)
            gain_ref[...] = jnp.broadcast_to(gain, (1, outs))
            sol_ref[...] += keep * direction[...]
        tree_sides(rounds)
        near_second(field, stage, leaf)
        acc[...] += near_dot(rounds, 3, 4)
        if rounds in LATE_TREE:
            near_finish(field, stage, leaf)
            acc[...] += near_dot(rounds, 4, 5)

        @pl.when(slices)
        def _():
            down_all(rounds, slicers - 1).wait_recv()

        @pl.when(jnp.logical_not(slices))
        def _():
            down_all(rounds, slicers).wait_recv()

        coupled = c_in[rounds].reshape(outs, rank)
        down = lax.dot_general(
            transfer_rows, coupled, (((1,), (1,)), ((), ())), preferred_element_type=f32
        )
        tree_wait(rounds, last_waits)
        level_one = jnp.dot(partners[...], skel[rounds], preferred_element_type=f32)
        far_part = jnp.dot(
            basis_p[...], (level_one + down).astype(bf16), preferred_element_type=f32
        )
        acc[...] += far_part
        if rounds not in LATE_TREE:
            near_finish(field, stage, leaf)
            acc[...] += near_dot(rounds, 4, 5)
        if rounds == ITERS - 1:
            break
        residual = res_ref[...] - acc[...]
        res_ref[...] = residual
        rho_next, keep, gain = momentum(sigma_ratio, spread, contraction)
        moved_on = keep * direction[...] + gain * residual
        direction[...] = moved_on
        sol_ref[...] += moved_on
        contraction = rho_next

    near_drain(points, 0, dim)

    @pl.when(slices)
    def _():
        tag_all(2 * slicers - 1).wait_send()
        for rounds in range(ITERS):
            down_all(rounds, n - 1).wait_send()

    @pl.when(jnp.logical_not(slices))
    def _():
        tag_all(2 * slicers).wait_send()

    for rounds in range(ITERS):
        near_drain(wide.at[rounds], rounds + 1, leaf)
        tree_drain(rounds)
        up_all(rounds, slicers).wait_send()


def fused_body(
    coords,
    right_side,
    leaf_perm,
    near_list,
    far_leaves,
    couplings,
    transfer,
    leaf_basis,
    cluster_of,
    far_clusters,
    cluster_couplings,
    ridge_weight,
):
    n = lax.axis_size("dev")
    leaf, dim = coords.shape
    outs = right_side.shape[1]
    rank = transfer.shape[1]
    clusters = cluster_couplings.shape[0]
    slicers = n // 2
    width = outs // slicers
    bf16, f32 = jnp.bfloat16, jnp.float32
    vmem = pl.BlockSpec(memory_space=pltpu.VMEM)
    hbm = pl.BlockSpec(memory_space=pltpu.HBM)
    sem = pltpu.SemaphoreType.DMA
    stages = ITERS + 1

    def stay(array):
        return pltpu.with_memory_space_constraint(array, pltpu.HBM)

    out = jax.ShapeDtypeStruct((leaf, outs), f32)
    base, residual, applied, gain = pl.pallas_call(
        functools.partial(fused_kernel, n),
        out_shape=(out, out, out, jax.ShapeDtypeStruct((1, outs), f32)),
        in_specs=[hbm] * 12,
        out_specs=(vmem, vmem, vmem, vmem),
        scratch_shapes=[
            pltpu.VMEM((5 * dim, leaf), f32),
            pltpu.VMEM((ITERS, 5 * leaf, outs), bf16),
            pltpu.VMEM((leaf, 5 * leaf), bf16),
            pltpu.VMEM((ITERS, n * rank, outs), bf16),
            pltpu.VMEM((ITERS, slicers, width, rank), bf16),
            pltpu.VMEM((ITERS, n, width, rank), bf16),
            pltpu.VMEM((2, n, 1, rank), f32),
            pltpu.VMEM((2 * n, 1, rank), f32),
            pltpu.VMEM((width, clusters * rank), bf16),
            pltpu.VMEM((clusters * rank, clusters * rank), bf16),
            pltpu.VMEM((rank, n * rank), bf16),
            pltpu.VMEM((ITERS, n, width, rank), bf16),
            pltpu.VMEM((ITERS, slicers, width, rank), bf16),
            pltpu.VMEM((leaf, rank), bf16),
            pltpu.VMEM((rank, leaf), bf16),
            pltpu.VMEM((leaf, 6 * dim), bf16),
            pltpu.VMEM((leaf, 128), f32),
            pltpu.VMEM((leaf, outs), f32),
            pltpu.VMEM(leaf_perm.shape, jnp.int32),
            pltpu.VMEM(leaf_basis.shape, bf16),
            pltpu.VMEM(transfer.shape, bf16),
            pltpu.VMEM(couplings.shape, bf16),
            pltpu.VMEM(cluster_couplings.shape, bf16),
            pltpu.VMEM((1, 1), f32),
            pltpu.SMEM((1, 1), jnp.int32),
            pltpu.SMEM(near_list.shape, jnp.int32),
            pltpu.SMEM(far_leaves.shape, jnp.int32),
            pltpu.SMEM(far_clusters.shape, jnp.int32),
            sem((12,)),
            sem((stages, 5, PARTS)),
            sem((stages, 5, PARTS)),
            sem((ITERS, 14)),
            sem((ITERS, n)),
            sem((2 * ITERS + 1,)),
            sem((2 * ITERS + 1,)),
        ],
        compiler_params=pltpu.CompilerParams(
            collective_id=0, has_side_effects=True, vmem_limit_bytes=48 << 20
        ),
        name="fused_solve",
    )(
        stay(coords.T),
        stay(right_side),
        stay(leaf_perm),
        stay(near_list),
        stay(far_leaves),
        stay(couplings),
        stay(transfer),
        stay(leaf_basis),
        cluster_of.reshape(1, 1),
        stay(far_clusters),
        stay(cluster_couplings),
        ridge_weight.reshape(1, 1),
    )
    residual = residual - applied
    return base + gain * residual, residual


def solution(mesh):
    fits = mesh.shape["grp"] == 2 and mesh.shape["dev"] % 4 == 0
    placed = (
        P(("grp", "dev"), None),
        P(("grp", "dev"), None),
        P(("grp", "dev"), None),
        P(("grp", "dev"), None),
        P(("grp", "dev"), None),
        P(("grp", "dev"), None, None, None),
        P(("grp", "dev"), None, None),
        P(("grp", "dev"), None),
        P(("grp", "dev")),
        P("grp", None),
        P("grp", None, None, None),
        P(),
    )
    return jax.shard_map(
        fused_body if fits else body,
        mesh=mesh,
        in_specs=placed,
        out_specs=(P(("grp", "dev"), None), P(("grp", "dev"), None)),
        check_vma=False,
    )
```
